512 devices in a mesh: seq: 128 (over y, z, core), mp: 4 (over x).
Axes of the slice: x: 4, y: 8, z: 8, core: 2. Of those that a mesh axis runs over, the one named last changes fastest.
Arguments:
- hidden_rows: bfloat16 [32768, 1536], P('seq', 'mp'), may hold values from -6 to 6
- norm_gain: bfloat16 [1536], P('mp'), may hold values from 0.099609375 to 1.8984375
- encodings: bfloat16 [256, 128, 1536], P('seq', None, 'mp'), may hold values from -56 to 56
- w_query: bfloat16 [1536, 1536], P('seq', 'mp'), may hold values from -0.15625 to 0.15625
- w_key: bfloat16 [1536, 1536], P('seq', 'mp'), may hold values from -0.15625 to 0.15625
- w_value: bfloat16 [1536, 1536], P('seq', 'mp'), may hold values from -0.625 to 0.625
- w_out: bfloat16 [1536, 1536], P('mp', 'seq'), may hold values from -0.4375 to 0.4375
- neighbours: int32 [512, 2], P('seq'), may hold values from 0 to 255, as said below
- grad_out: bfloat16 [32768, 1536], P('seq', 'mp'), may hold values from -6 to 6
Outputs:
- branch_out: bfloat16 [32768, 1536], P('seq', 'mp')
- grad_rows: bfloat16 [32768, 1536], P('seq', 'mp')
- grad_encodings: bfloat16 [256, 128, 1536], P('seq', None, 'mp')
The draws below stay inside these ranges and needn't reach their ends.
Inputs may be any that keep to these rules, and one draw needn't show every extreme that they name: `neighbours`: A stretch of seq device d names only encoded stretches whose owner, id // 2, is one of the devices d - 2 to d + 2 along seq, counted around the axis. On every device the first stretch names an encoded stretch of owner d - 2 first and, second, the last encoded stretch (local index 1) of owner d + 2.
All inputs are finite; a program needn't handle non-finite values.
Results may differ from the reference program's by a relative error of at most 0.023.
The reference program's roundings to bfloat16 on the way (of `normed`, `queries`, `weights_low`, `attended`, `d_attended`, `d_scores` and `d_queries`) count: a program that leaves them out, or rounds other values in their place, can miss the bound.
Values may be sent and summed in bfloat16 or wider, within the bound.
A program may use at most 64 MiB of HBM per device.

```python
import jax
import jax.numpy as jnp
from jax import lax

D = 1536
HEADS = 12
HD = 128
STRETCH = 64
NBR = 2
RET = 128
SPAN = 2
CH_DEV = 4
OWN_DEV = 2
STRETCHES = 512
TOKENS = 32768
BASE = 256
N_MP = 4


def draw_encodings(key, part):
    first_key = jax.random.fold_in(key, 0)
    return jnp.clip(jax.random.normal(first_key, (BASE, RET, D), jnp.float32), -6.0, 6.0).astype(jnp.bfloat16)


def draw_neighbours(key, part):
    split_keys = jax.random.split(key, 4)
    device_count = STRETCHES // CH_DEV
    span_width = 2 * SPAN + 1
    offsets = jnp.minimum(jax.random.randint(split_keys[0], (STRETCHES, NBR), 0, span_width), jax.random.randint(split_keys[1], (STRETCHES, NBR), 0, span_width)) - SPAN
    local_index = jnp.minimum(jax.random.randint(split_keys[2], (STRETCHES, NBR), 0, OWN_DEV), jax.random.randint(split_keys[3], (STRETCHES, NBR), 0, OWN_DEV))
    leading = (jnp.arange(STRETCHES) % CH_DEV == 0)[:, None]
    column = jnp.arange(NBR)[None, :]
    forced = jnp.where(column == 0, -SPAN, SPAN)
    offsets = jnp.where(leading, forced, offsets)
    local_index = jnp.where(leading & (column == 1), OWN_DEV - 1, local_index)
    device = (jnp.arange(STRETCHES) // CH_DEV)[:, None]
    owner = (device + offsets) % device_count
    return (owner * OWN_DEV + local_index).astype(jnp.int32)


def block_scale(key, dims, shards, low, high):
    loudness = 1.0
    for position, shards_of in shards:
        draws = jax.random.uniform(jax.random.fold_in(jax.random.fold_in(key, 6), position), (shards_of,), jnp.float32, low / len(shards), high / len(shards))
        loudness = loudness * jnp.repeat(jnp.exp(draws), dims[position] // shards_of).reshape((-1,) + (1,) * (len(dims) - 1 - position))
    return loudness


def scatter_about(own_key, extent, deviation, reach, shards=(), dtype=jnp.bfloat16):
    result = jax.random.normal(own_key, extent, jnp.float32) * deviation
    if len(shards) > 0:
        result = block_scale(own_key, extent, shards, -0.22, 0.18) * result
    return jnp.clip(result, min=-reach, max=reach).astype(dtype)


def setup_inputs(seed: int = 0) -> dict:
    keys = jax.random.split(jax.random.key(seed), 10)
    hidden_rows = scatter_about(keys[0], (TOKENS, D), 1.0, 6.0, ((0, 128), (1, 4)))
    norm_gain = jnp.clip(1.0 + 0.18 * jax.random.normal(keys[1], (D,), jnp.float32), 0.099609375, 1.8984375).astype(jnp.bfloat16)
    encodings = draw_encodings(jax.random.fold_in(keys[9], 71), 0)
    w_query = scatter_about(keys[3], (D, D), D ** -0.5, 0.15625, ((0, 128), (1, 4)))
    w_key = scatter_about(keys[4], (D, D), D ** -0.5, 0.15625, ((0, 128), (1, 4)))
    w_value = scatter_about(keys[5], (D, D), (D // 16) ** -0.5, 0.625, ((0, 128), (1, 4)))
    w_out = scatter_about(keys[6], (D, D), (D // 8) ** -0.5, 0.4375, ((0, 4), (1, 128)))
    neighbours = draw_neighbours(jax.random.fold_in(keys[9], 71), 0)
    grad_out = scatter_about(keys[8], (TOKENS, D), 1.0, 6.0, ((0, 128), (1, 4)))
    return {"hidden_rows": hidden_rows, "norm_gain": norm_gain, "encodings": encodings, "w_query": w_query, "w_key": w_key, "w_value": w_value, "w_out": w_out, "neighbours": neighbours, "grad_out": grad_out}


epsilon = 1e-05

def round_low(values):
    return lax.optimization_barrier(values.astype(jnp.bfloat16)).astype(jnp.float32)

def grouped_sum(left, right, transpose_right):
    group_width = D // N_MP
    summed = jnp.zeros((left.shape[0], D), jnp.float32)
    for group in range(N_MP):
        begin = group * group_width
        left_part = left[:, begin:begin + group_width]
        if transpose_right:
            right_part = right[:, begin:begin + group_width].T
        else:
            right_part = right[begin:begin + group_width, :]
        summed = summed + round_low(jnp.dot(left_part, right_part, preferred_element_type=jnp.float32))
    return summed

def reference(hidden_rows, norm_gain, encodings, w_query, w_key, w_value, w_out, neighbours, grad_out):
    rows_float = hidden_rows.astype(jnp.float32)
    gain_float = norm_gain.astype(jnp.float32)
    inv_rms = lax.rsqrt(lax.optimization_barrier(jnp.mean(rows_float * rows_float, axis=1, keepdims=True)) + epsilon)
    normed = (rows_float * inv_rms * gain_float).astype(jnp.bfloat16)
    queries = jnp.dot(normed, w_query, preferred_element_type=jnp.float32).astype(jnp.bfloat16)
    enc_flat = encodings.reshape(BASE * RET, D)
    key_table = jnp.dot(enc_flat, w_key, preferred_element_type=jnp.float32).astype(jnp.bfloat16).reshape(BASE, RET, HEADS, HD)
    value_table = jnp.dot(enc_flat, w_value, preferred_element_type=jnp.float32).astype(jnp.bfloat16).reshape(BASE, RET, HEADS, HD)
    d_attended = jnp.dot(grad_out, w_out.T, preferred_element_type=jnp.float32).astype(jnp.bfloat16)
    score_scale = HD ** (-0.5)

    def one_stretch(carry, item):
        key_grads, value_grads = carry
        query_block, grad_block, chosen = item
        key_rows = key_table[chosen].reshape(NBR * RET, HEADS, HD).astype(jnp.float32)
        value_rows = value_table[chosen].reshape(NBR * RET, HEADS, HD).astype(jnp.float32)
        query_float = query_block.astype(jnp.float32)
        grad_float = grad_block.astype(jnp.float32)
        scores = jnp.einsum('mhe,she->hms', query_float, key_rows) * score_scale
        row_peak = lax.optimization_barrier(jnp.max(scores, axis=2, keepdims=True))
        exponent = jnp.exp(scores - row_peak)
        weights = exponent / lax.optimization_barrier(jnp.sum(exponent, axis=2, keepdims=True))
        weights_low = round_low(weights)
        attended = jnp.einsum('hms,she->mhe', weights_low, value_rows).astype(jnp.bfloat16)
        d_weights = jnp.einsum('mhe,she->hms', grad_float, value_rows)
        d_scores = round_low(weights * (d_weights - lax.optimization_barrier(jnp.sum(d_weights * weights, axis=2, keepdims=True))) * score_scale)
        d_queries = jnp.einsum('hms,she->mhe', d_scores, key_rows).astype(jnp.bfloat16)
        d_keys = jnp.einsum('hms,mhe->she', d_scores, query_float).reshape(NBR, RET, HEADS, HD)
        d_values = jnp.einsum('hms,mhe->she', weights_low, grad_float).reshape(NBR, RET, HEADS, HD)
        key_grads = key_grads.at[chosen].add(d_keys)
        value_grads = value_grads.at[chosen].add(d_values)
        return ((key_grads, value_grads), (attended, d_queries))
    zeros_table = jnp.zeros((BASE, RET, HEADS, HD), jnp.float32)
    items = (queries.reshape(STRETCHES, STRETCH, HEADS, HD), d_attended.reshape(STRETCHES, STRETCH, HEADS, HD), neighbours.astype(jnp.int32))
    (key_grads, value_grads), (attended, d_queries) = lax.scan(one_stretch, (zeros_table, zeros_table), items)
    attended = attended.reshape(TOKENS, D)
    d_queries = d_queries.reshape(TOKENS, D)
    branch_out = grouped_sum(attended, w_out, False).astype(jnp.bfloat16)
    d_normed = grouped_sum(d_queries, w_query, True)
    statistic = lax.optimization_barrier(jnp.mean(rows_float * gain_float * d_normed, axis=1, keepdims=True))
    grad_rows = (inv_rms * gain_float * d_normed - rows_float * inv_rms ** 3 * statistic).astype(jnp.bfloat16)
    key_low = key_grads.astype(jnp.bfloat16).reshape(BASE * RET, D)
    value_low = value_grads.astype(jnp.bfloat16).reshape(BASE * RET, D)
    group_width = D // N_MP
    enc_summed = jnp.zeros((BASE * RET, D), jnp.float32)
    for group in range(N_MP):
        begin = group * group_width
        product = jnp.dot(key_low[:, begin:begin + group_width], w_key[:, begin:begin + group_width].T, preferred_element_type=jnp.float32)
        product = product + jnp.dot(value_low[:, begin:begin + group_width], w_value[:, begin:begin + group_width].T, preferred_element_type=jnp.float32)
        enc_summed = enc_summed + round_low(product)
    grad_encodings = enc_summed.astype(jnp.bfloat16).reshape(BASE, RET, D)
    return (branch_out, grad_rows, grad_encodings)
```

```python
import jax
import jax.numpy as jnp
import numpy as np
from jax import lax
from jax.experimental import pallas as pl
from jax.experimental.pallas import tpu as pltpu
from jax.sharding import PartitionSpec as P

HD = 128
STRETCH = 64
RET = 128
SPAN = 2
OWN_DEV = 2
NY = 8
NZ = 8
N_MP = 4
HEADS = 3
WIN = 2 * SPAN + 1
SLOTS = WIN * OWN_DEV
W = 384
D = 1536
SHARD = 12
PAD = 16
T = 256
CH = 4
F32 = jnp.float32
BF16 = jnp.bfloat16
MESH = pl.DeviceIdType.MESH
NT = (((1,), (1,)), ((), ()))
TN = (((0,), (0,)), ((), ()))
epsilon = 1e-05


def order_matrix():
    rows = np.arange(2 * 16 * SHARD)
    weight, rest = rows // (16 * SHARD), rows % (16 * SHARD)
    source = (rest // SHARD) * 2 * PAD + weight * PAD + rest % SHARD
    return (np.arange(2 * 16 * PAD)[None, :] == source[:, None]).astype(np.float32)


def kernel(
    slot_ref, hid_ref, grad_ref, enc_ref, gain_ref, ws_ref, perm_ref,
    bout_ref, grow_ref, genc_ref,
    gx, gg, stage, panel, nx, inv, acc, qs, da, win, wts, wl, ds, qm, dwin, own, rg,
    att, dq, low, sb, rb, mine, st, so, outs,
    z_send, z_recv, x_send, x_recv, g_send, g_recv, r_send, r_recv, b_send, b_recv,
    k_send, k_recv, v_send, v_recv, p_send, p_recv, s_send, s_recv, loc, osem,
):
    s_id = lax.axis_index("seq")
    m_id = lax.axis_index("mp")
    core = lax.rem(s_id, 2)
    z_id = lax.rem(s_id // 2, NZ)
    y_id = s_id // (2 * NZ)

    def sid(y, z, c):
        return (lax.rem(y + NY, NY) * NZ + lax.rem(z + NZ, NZ)) * 2 + lax.rem(c, 2)

    def near(o):
        return lax.rem(s_id + o + 2 * NY * NZ, 2 * NY * NZ)

    def remote(src, dst, ssem, rsem, seq, mp):
        return pltpu.make_async_remote_copy(
            src_ref=src, dst_ref=dst, send_sem=ssem, recv_sem=rsem,
            device_id=(seq, mp), device_id_type=MESH,
        )

    z_peers = [(dz, dc) for dz in range(NZ) for dc in range(2) if (dz, dc) != (0, 0)]
    barrier = pltpu.get_barrier_semaphore()
    greeted = [(sid(y_id, z_id + dz, core + dc), m_id) for dz, dc in z_peers]
    greeted += [(sid(y_id + 1, z_id, core), m_id), (sid(y_id - 1, z_id, core), m_id)]
    greeted += [(near(o), m_id) for o in (-2, -1, 1, 2)]
    greeted += [(s_id, lax.rem(m_id + dm, N_MP)) for dm in (1, 2, 3)]
    for who in greeted:
        pl.semaphore_signal(barrier, inc=1, device_id=who, device_id_type=MESH)
    pl.semaphore_wait(barrier, len(greeted))

    sends = []

    def go(copy):
        copy.start()
        sends.append(copy)

    shard_rows = pl.ds(pl.multiple_of((z_id * 2 + core) * 2 * PAD, 2 * PAD), 2 * PAD)
    for dz, dc in z_peers:
        k = dz * 2 + dc
        go(remote(ws_ref.at[lax.rem(core + dc, 2)], stage.at[shard_rows], z_send.at[k], z_recv.at[k],
                  sid(y_id, z_id + dz, core + dc), m_id))
    own_shard = pltpu.make_async_copy(ws_ref.at[core], stage.at[shard_rows], loc.at[0])
    own_shard.start()

    locals_ = []
    for t, ref in ((0, enc_ref), (1, grad_ref), (2, hid_ref)):
        for dm in (1, 2, 3):
            go(remote(ref, gx.at[t, m_id], x_send.at[t, dm], x_recv.at[t, dm],
                      s_id, lax.rem(m_id + dm, N_MP)))
        c = pltpu.make_async_copy(ref, gx.at[t, m_id], loc.at[1 + t])
        c.start()
        locals_.append(c)
    for dm in (1, 2, 3):
        go(remote(gain_ref, gg.at[m_id], g_send.at[dm], g_recv.at[dm],
                  s_id, lax.rem(m_id + dm, N_MP)))
    gain_copy = pltpu.make_async_copy(gain_ref, gg.at[m_id], loc.at[4])
    gain_copy.start()

    def got_x(t):
        locals_[t].wait()
        for dm in (1, 2, 3):
            remote(gx.at[t, 0], gx.at[t, 0], x_send.at[t, dm], x_recv.at[t, dm], s_id, m_id).wait_recv()

    own_shard.wait()
    for dz, dc in z_peers:
        k = dz * 2 + dc
        remote(stage.at[pl.ds(0, 2 * PAD)], stage.at[pl.ds(0, 2 * PAD)], z_send.at[k], z_recv.at[k],
               s_id, m_id).wait_recv()
    ordered = jnp.dot(perm_ref[...], stage[...], preferred_element_type=F32).astype(BF16)
    half = 16 * SHARD
    panel[2 * core, y_id] = ordered[:half]
    panel[2 * core + 1, y_id] = ordered[half:]

    def chunk(k):
        return lax.rem(y_id + k + NY, NY)

    def ring(i, k, step, right):
        place = panel.at[2 * core + i, chunk(k)]
        e = step * 2 + right
        to = sid(y_id + (1 if right else -1), z_id, core)
        return remote(place, place, r_send.at[i, e], r_recv.at[i, e], to, m_id)

    def share(i, k):
        place = panel.at[2 * core + i, chunk(k)]
        go(remote(place, place, b_send.at[i, k % NY], b_recv.at[i, k % NY], sid(y_id, z_id, core + 1), m_id))

    def last(i, right):
        return 4 if right == (i == 0) else 3

    def ring_start(i):
        go(ring(i, 0, 1, 1))
        go(ring(i, 0, 1, 0))
        share(i, 0)

    def ring_step(i, step):
        for right in (1, 0):
            if step <= last(i, right):
                k = -step if right else step
                ring(i, k, step, right).wait_recv()
                if step < last(i, right):
                    go(ring(i, k, step + 1, right))
                share(i, k)

    def got_shared(i):
        for k in range(NY):
            place = panel.at[2 * core + i, k]
            remote(place, place, b_send.at[i, k], b_recv.at[i, k], s_id, m_id).wait_recv()

    ring_start(0)
    ring_step(0, 1)
    ring_start(1)

    got_x(2)
    gain_copy.wait()
    for dm in (1, 2, 3):
        remote(gg.at[0], gg.at[0], g_send.at[dm], g_recv.at[dm], s_id, m_id).wait_recv()

    ring_step(0, 2)

    @pl.loop(0, 4)
    def _(b):
        rows = pl.ds(pl.multiple_of(b * 64, 64), 64)
        total = jnp.zeros((64, HD), F32)
        for mm in range(N_MP):
            x = gx[2, mm, rows, :].astype(F32)
            x = x * x
            total = total + (x[:, :128] + x[:, 128:256] + x[:, 256:])
        scale = lax.rsqrt(jnp.sum(total, axis=1, keepdims=True) * (1.0 / D) + epsilon)
        inv[rows, :] = jnp.broadcast_to(scale, (64, HD))
        for mm in range(N_MP):
            x = gx[2, mm, rows, :].astype(F32)
            nx[mm, rows, :] = (x * scale * gg[mm, 0:1, :]).astype(BF16)

    ring_step(1, 1)
    ring_step(0, 3)
    ring_step(1, 2)
    ring_step(0, 4)
    ring_step(1, 3)
    got_shared(0)

    def block(w, mm):
        return panel[w, pl.ds(2 * mm, 2)].reshape(W, W)

    def project(x, w):
        for mm in range(N_MP):
            part = jnp.dot(x[mm], block(w, mm), preferred_element_type=F32)
            if mm == 0:
                acc[...] = part
            else:
                acc[...] += part
        return acc[...].astype(BF16)

    got_x(0)
    for kv, w in ((0, 0), (1, 2)):
        win[SPAN, kv] = project(gx.at[0], w).reshape(OWN_DEV, RET, W)
        for o in (-2, 2, -1, 1):
            go(remote(win.at[SPAN, kv], win.at[SPAN - o, kv], k_send.at[kv, SPAN + o],
                      k_recv.at[kv, SPAN - o], near(o), m_id))

    ring_step(1, 4)
    got_shared(1)
    got_x(1)
    da[...] = project(gx.at[1], 1)
    qs[...] = project(nx, 3)

    for kv in (0, 1):
        for o in (-2, 2, -1, 1):
            place = win.at[SPAN, kv]
            remote(place, place, k_send.at[kv, SPAN + o], k_recv.at[kv, SPAN + o], s_id, m_id).wait_recv()

    score_scale = HD ** (-0.5)

    def rows_of(kv, c, h):
        cols = pl.ds(h * HD, HD)
        parts = []
        for j in range(2):
            slot = slot_ref[2 * c + j]
            parts.append(win[slot // 2, kv, slot % 2, :, cols])
        return jnp.concatenate(parts, axis=0)

    pairs = [(c, h) for c in range(CH) for h in range(HEADS)]
    for c, h in pairs:
        r, cols = pl.ds(c * STRETCH, STRETCH), pl.ds(h * HD, HD)
        scores = lax.dot_general(qs[r, cols], rows_of(0, c, h), NT, preferred_element_type=F32) * score_scale
        e = jnp.exp(scores - jnp.max(scores, axis=1, keepdims=True))
        weights = e / jnp.sum(e, axis=1, keepdims=True)
        wts[c * HEADS + h] = weights
        weights_low = weights.astype(BF16)
        for j in range(2):
            wl[h, j, r, :] = weights_low[:, j * RET:(j + 1) * RET]
        att[r, cols] = jnp.dot(weights_low, rows_of(1, c, h), preferred_element_type=F32).astype(BF16)

    def send_piece(b, dm, piece):
        if dm == 0:
            mine[b] = piece
        else:
            sb[b, dm - 1] = piece
            go(remote(sb.at[b, dm - 1], rb.at[b, dm - 1], p_send.at[b, dm], p_recv.at[b, dm],
                      s_id, lax.rem(m_id + dm, N_MP)))

    def gather_piece(b):
        for dm in (1, 2, 3):
            remote(sb.at[b, 0], rb.at[b, 0], p_send.at[b, dm], p_recv.at[b, dm], s_id, m_id).wait_recv()

    for dm in (2, 1, 3, 0):
        to = lax.rem(m_id + dm, N_MP)
        piece = lax.dot_general(att[...], block(1, to), NT, preferred_element_type=F32)
        send_piece(0, dm, piece.astype(BF16))

    for c, h in pairs:
        r, cols = pl.ds(c * STRETCH, STRETCH), pl.ds(h * HD, HD)
        weights = wts[c * HEADS + h]
        d_weights = lax.dot_general(da[r, cols], rows_of(1, c, h), NT, preferred_element_type=F32)
        inner = jnp.sum(d_weights * weights, axis=1, keepdims=True)
        d_scores = (weights * (d_weights - inner) * score_scale).astype(BF16)
        for j in range(2):
            ds[h, j, r, :] = d_scores[:, j * RET:(j + 1) * RET]
        dq[r, cols] = jnp.dot(d_scores, rows_of(0, c, h), preferred_element_type=F32).astype(BF16)

    for kv, left, right in ((0, ds, qs), (1, wl, da)):
        for h in range(HEADS):
            cols = pl.ds(h * HD, HD)
            for c in range(CH):
                rows = right[pl.ds(c * STRETCH, STRETCH), cols]
                for j in range(2):
                    slot = slot_ref[2 * c + j]
                    for s in range(SLOTS):
                        keep = (slot == s).astype(F32).astype(BF16)
                        qm[pl.ds(j * T + c * STRETCH, STRETCH), pl.ds(s * HD, HD)] = rows * keep
            grads = lax.dot_general(left[h].reshape(2 * T, RET), qm[...], TN, preferred_element_type=F32)
            for s in range(SLOTS):
                part = grads[:, s * HD:(s + 1) * HD]
                if s // 2 == SPAN:
                    own[kv, s % 2, :, cols] = part
                else:
                    dwin[s // 2, kv, s % 2, :, cols] = part.astype(BF16)
        for o in (-2, 2, -1, 1):
            go(remote(dwin.at[SPAN + o, kv], rg.at[SPAN - o, kv], v_send.at[kv, SPAN + o],
                      v_recv.at[kv, SPAN - o], near(o), m_id))

    acc[:, :HD] = jnp.zeros((T, HD), F32)
    for dm in (2, 1, 3, 0):
        to = lax.rem(m_id + dm, N_MP)
        piece = lax.dot_general(dq[...], block(3, to), NT, preferred_element_type=F32).astype(BF16)
        send_piece(1, dm, piece)
        prod = gx[2, to].astype(F32) * gg[to, 0:1, :] * piece.astype(F32)
        acc[:, :HD] += prod[:, :128] + prod[:, 128:256] + prod[:, 256:]
    st[...] = jnp.broadcast_to(jnp.sum(acc[:, :HD].T, axis=0, keepdims=True), (8, T))
    for dm in (1, 2, 3):
        go(remote(st, so.at[dm - 1], s_send.at[dm], s_recv.at[dm], s_id, lax.rem(m_id + dm, N_MP)))

    def total(b, rows):
        value = mine[b, rows, :].astype(F32)
        for i in range(3):
            value = value + rb[b, i, rows, :].astype(F32)
        return value

    gather_piece(0)

    @pl.loop(0, 4)
    def _(b):
        rows = pl.ds(pl.multiple_of(b * 64, 64), 64)
        outs[0, rows, :] = total(0, rows).astype(BF16)

    out0 = pltpu.make_async_copy(outs.at[0], bout_ref, osem.at[0])
    out0.start()

    for kv in (0, 1):
        for o in (-2, 2, -1, 1):
            place = rg.at[SPAN, kv]
            remote(place, place, v_send.at[kv, SPAN + o], v_recv.at[kv, SPAN + o], s_id, m_id).wait_recv()
        for l in range(OWN_DEV):
            value = own[kv, l]
            for w in (0, 1, 3, 4):
                value = value + rg[w, kv, l].astype(F32)
            low[kv, pl.ds(l * RET, RET), :] = value.astype(BF16)
    for dm in (2, 1, 3, 0):
        to = lax.rem(m_id + dm, N_MP)
        acc[...] = lax.dot_general(low[0], block(0, to), NT, preferred_element_type=F32)
        acc[...] += lax.dot_general(low[1], block(2, to), NT, preferred_element_type=F32)
        send_piece(2, dm, acc[...].astype(BF16))

    gather_piece(1)
    for dm in (1, 2, 3):
        remote(st, so.at[dm - 1], s_send.at[dm], s_recv.at[dm], s_id, m_id).wait_recv()
    stat = st[0:1, :] + so[0, 0:1, :] + so[1, 0:1, :] + so[2, 0:1, :]
    acc[:, :HD] = jnp.broadcast_to(stat * (1.0 / D), (HD, T)).T

    @pl.loop(0, 4)
    def _(b):
        rows = pl.ds(pl.multiple_of(b * 64, 64), 64)
        d_normed = total(1, rows)
        scale = inv[rows, :]
        scale = jnp.concatenate([scale] * 3, axis=1)
        mean = acc[rows, :HD]
        mean = jnp.concatenate([mean] * 3, axis=1)
        x = gx[2, m_id, rows, :].astype(F32)
        value = scale * gg[m_id, 0:1, :] * d_normed - x * (scale * scale * scale) * mean
        outs[1, rows, :] = value.astype(BF16)

    out1 = pltpu.make_async_copy(outs.at[1], grow_ref, osem.at[1])
    out1.start()

    gather_piece(2)

    @pl.loop(0, 4)
    def _(b):
        rows = pl.ds(pl.multiple_of(b * 64, 64), 64)
        outs[2, rows, :] = total(2, rows).astype(BF16)

    out2 = pltpu.make_async_copy(outs.at[2], genc_ref, osem.at[2])
    out2.start()
    for copy in sends:
        copy.wait_send()
    out0.wait()
    out1.wait()
    out2.wait()


def layer(slots, hidden_rows, grad_out, encodings, gain, stacked, perm):
    dma = pltpu.SemaphoreType.DMA
    v = pltpu.VMEM
    any_ = pl.BlockSpec(memory_space=pl.ANY)
    out = jax.ShapeDtypeStruct((T, W), BF16)
    return pl.pallas_call(
        kernel,
        out_shape=(out, out, out),
        in_specs=[pl.BlockSpec(memory_space=pltpu.SMEM)] + [any_] * 5 + [pl.BlockSpec(memory_space=pltpu.VMEM)],
        out_specs=(any_, any_, any_),
        scratch_shapes=[
            v((3, N_MP, T, W), BF16),
            v((N_MP, 8, W), F32),
            v((16 * 2 * PAD, W), BF16),
            v((4, NY, 16 * SHARD, W), BF16),
            v((N_MP, T, W), BF16),
            v((T, HD), F32),
            v((T, W), F32),
            v((T, W), BF16),
            v((T, W), BF16),
            v((WIN, 2, OWN_DEV, RET, W), BF16),
            v((CH * HEADS, STRETCH, 2 * RET), F32),
            v((HEADS, 2, T, RET), BF16),
            v((HEADS, 2, T, RET), BF16),
            v((2 * T, SLOTS * HD), BF16),
            v((WIN, 2, OWN_DEV, RET, W), BF16),
            v((2, OWN_DEV, RET, W), F32),
            v((WIN, 2, OWN_DEV, RET, W), BF16),
            v((T, W), BF16),
            v((T, W), BF16),
            v((2, T, W), BF16),
            v((3, 3, T, W), BF16),
            v((3, 3, T, W), BF16),
            v((3, T, W), BF16),
            v((8, T), F32),
            v((3, 8, T), F32),
            v((3, T, W), BF16),
            dma((16,)), dma((16,)),
            dma((3, 4)), dma((3, 4)),
            dma((4,)), dma((4,)),
            dma((2, 10)), dma((2, 10)),
            dma((2, NY)), dma((2, NY)),
            dma((2, WIN)), dma((2, WIN)),
            dma((2, WIN)), dma((2, WIN)),
            dma((3, 4)), dma((3, 4)),
            dma((4,)), dma((4,)),
            dma((5,)), dma((3,)),
        ],
        compiler_params=pltpu.CompilerParams(
            collective_id=0, has_side_effects=True, vmem_limit_bytes=56 << 20
        ),
    )(slots, hidden_rows, grad_out, encodings, gain, stacked, perm)


def shards(hidden_rows, norm_gain, encodings, w_query, w_key, w_value, w_out, neighbours, grad_out):
    device = lax.axis_index("seq")
    owners = neighbours // OWN_DEV
    offsets = (owners - device + SPAN) % lax.axis_size("seq")
    slots = (offsets * OWN_DEV + neighbours % OWN_DEV).reshape(-1)
    stacked = jnp.stack([w_key, w_out.T, w_value, w_query], axis=0)
    stacked = jnp.pad(stacked, ((0, 0), (0, PAD - SHARD), (0, 0))).reshape(2, 2 * PAD, W)
    gain = jnp.broadcast_to(norm_gain.astype(F32)[None, :], (8, W))
    perm = jnp.asarray(order_matrix(), BF16)
    bout, grow, genc = layer(
        slots, hidden_rows, grad_out, encodings.reshape(T, W), gain, stacked, perm
    )
    return bout, grow, genc.reshape(OWN_DEV, RET, W)


def solution(mesh):
    placed = (
        P("seq", "mp"),
        P("mp"),
        P("seq", None, "mp"),
        P("seq", "mp"),
        P("seq", "mp"),
        P("seq", "mp"),
        P("mp", "seq"),
        P("seq", None),
        P("seq", "mp"),
    )
    return jax.shard_map(
        shards,
        mesh=mesh,
        in_specs=placed,
        out_specs=(P("seq", "mp"), P("seq", "mp"), P("seq", None, "mp")),
        check_vma=False,
    )
```

```python
import jax
import jax.numpy as jnp
import numpy as np
from jax import lax
from jax.experimental import pallas as pl
from jax.experimental.pallas import tpu as pltpu
from jax.sharding import PartitionSpec as P

HD = 128
STRETCH = 64
RET = 128
SPAN = 2
OWN_DEV = 2
NY = 8
NZ = 8
N_MP = 4
HEADS = 3
WIN = 2 * SPAN + 1
SLOTS = WIN * OWN_DEV
W = 384
D = 1536
SHARD = 12
PAD = 16
HALF = 96
T = 256
CH = 4
F32 = jnp.float32
BF16 = jnp.bfloat16
MESH = pl.DeviceIdType.MESH
NT = (((1,), (1,)), ((), ()))
TN = (((0,), (0,)), ((), ()))
epsilon = 1e-05


def order_matrices():
    rows = np.arange(16 * SHARD)
    columns = np.arange(2 * W // 3)[None, :]
    padded = (rows // SHARD) * PAD + rows % SHARD
    pair = 2 * SHARD
    even = (rows // pair) * 32 + rows % pair
    return np.stack([columns == source[:, None] for source in (padded, even, even + 8)]).astype(np.float32)


def kernel(
    slot_ref, hid_ref, grad_ref, enc_ref, gain_ref, ws_ref, perm_ref,
    bout_ref, grow_ref, genc_ref,
    gx, gg, pair, stage, panel, ordered, nx, inv, acc, qs, da, win, wts, wl, ds, qm, dwin, own, rs, dsum, rg,
    att, dq, low, sb, rly, rb, mine, st, so, outs,
    a_send, a_recv, z_send, z_recv, x_send, x_recv, g_send, g_recv, r_send, r_recv, b_send, b_recv,
    k_send, k_recv, v_send, v_recv, p_send, p_recv, s_send, s_recv, loc, osem,
):
    s_id = lax.axis_index("seq")
    m_id = lax.axis_index("mp")
    core = lax.rem(s_id, 2)
    z_id = lax.rem(s_id // 2, NZ)
    y_id = s_id // (2 * NZ)

    def sid(y, z, c):
        return (lax.rem(y + NY, NY) * NZ + lax.rem(z + NZ, NZ)) * 2 + lax.rem(c, 2)

    def near(o):
        return lax.rem(s_id + o + 2 * NY * NZ, 2 * NY * NZ)

    def remote(src, dst, ssem, rsem, seq, mp):
        return pltpu.make_async_remote_copy(
            src_ref=src, dst_ref=dst, send_sem=ssem, recv_sem=rsem,
            device_id=(seq, mp), device_id_type=MESH,
        )

    barrier = pltpu.get_barrier_semaphore()
    sibling = sid(y_id, z_id, core + 1)
    place_of = (z_id, y_id)

    def peer(i, e):
        return sid(y_id, z_id + e, core) if i == 0 else sid(y_id + e, z_id, core)

    greeted = [(sibling, m_id)]
    greeted += [(peer(i, e), m_id) for i in (0, 1) for e in range(1, NZ)]
    greeted += [(near(2), m_id), (near(-2), m_id)]
    greeted += [(s_id, lax.rem(m_id + dm, N_MP)) for dm in (1, 2, 3)]
    for who in greeted:
        pl.semaphore_signal(barrier, inc=1, device_id=who, device_id_type=MESH)
    pl.semaphore_wait(barrier, len(greeted))

    sends = []

    def go(copy):
        copy.start()
        sends.append(copy)

    own_shards = []
    for i in (0, 1):
        go(remote(ws_ref.at[1 - core, i], pair.at[i, core], a_send.at[i], a_recv.at[i], sibling, m_id))
        c = pltpu.make_async_copy(ws_ref.at[core, i], pair.at[i, core], loc.at[5 + i])
        c.start()
        own_shards.append(c)

    locals_ = {}
    for t, ref in ((0, enc_ref), (2, hid_ref), (1, grad_ref)):
        for dm in (1, 2, 3):
            go(remote(ref, gx.at[t, m_id], x_send.at[t, dm], x_recv.at[t, dm],
                      s_id, lax.rem(m_id + dm, N_MP)))
        c = pltpu.make_async_copy(ref, gx.at[t, m_id], loc.at[1 + t])
        c.start()
        locals_[t] = c
    for dm in (1, 2, 3):
        go(remote(gain_ref, gg.at[m_id], g_send.at[dm], g_recv.at[dm],
                  s_id, lax.rem(m_id + dm, N_MP)))
    gain_copy = pltpu.make_async_copy(gain_ref, gg.at[m_id], loc.at[4])
    gain_copy.start()

    def got_x(t):
        locals_[t].wait()
        for dm in (1, 2, 3):
            remote(gx.at[t, 0], gx.at[t, 0], x_send.at[t, dm], x_recv.at[t, dm], s_id, m_id).wait_recv()

    for i in (0, 1):
        own_shards[i].wait()
        remote(pair.at[i, 0], pair.at[i, 0], a_send.at[i], a_recv.at[i], s_id, m_id).wait_recv()
        for e in (1, 7, 2, 6, 3, 5, 4):
            go(remote(pair.at[i], stage.at[i, place_of[i]], z_send.at[i, e], z_recv.at[i, e], peer(i, e), m_id))
        stage[i, place_of[i]] = pair[i]

    def ring(i, sub, k, step, right):
        place = panel.at[2 * core + i, lax.rem(place_of[1 - i] + k + NY, NY), pl.ds(sub * HALF, HALF)]
        e = step * 2 + right
        return remote(place, place, r_send.at[i, sub, e], r_recv.at[i, sub, e],
                      peer(1 - i, 1 if right else -1), m_id)

    def share(i, k):
        place = panel.at[2 * core + i, lax.rem(place_of[1 - i] + k + NY, NY)]
        go(remote(place, place, b_send.at[i, k % NY], b_recv.at[i, k % NY], sibling, m_id))

    def last(sub, right):
        return 4 if right == (sub == 0) else 3

    def ring_start(i):
        for e in range(1, NZ):
            remote(pair.at[i], stage.at[i, 0], z_send.at[i, e], z_recv.at[i, e], s_id, m_id).wait_recv()
        panel[2 * core + i, place_of[1 - i]] = jnp.dot(
            perm_ref[0], stage[i].reshape(16 * PAD, W), preferred_element_type=F32
        ).astype(BF16)
        for sub in (0, 1):
            go(ring(i, sub, 0, 1, 1))
            go(ring(i, sub, 0, 1, 0))
        share(i, 0)

    def ring_step(i, step):
        for right in (1, 0):
            k = -step if right else step
            for sub in (0, 1):
                if step <= last(sub, right):
                    ring(i, sub, k, step, right).wait_recv()
                    if step < last(sub, right):
                        go(ring(i, sub, k, step + 1, right))
            if step < 4 or right == 0:
                share(i, k)

    def got_shared(i):
        for k in range(NY):
            place = panel.at[2 * core + i, k]
            remote(place, place, b_send.at[i, k], b_recv.at[i, k], s_id, m_id).wait_recv()

    ring_start(0)
    ring_start(1)
    for step in (1, 2, 3, 4):
        ring_step(0, step)
        if step < 4:
            ring_step(1, step)
    got_shared(0)

    def block(w, mm):
        if w in (1, 3):
            return ordered[w // 2, pl.ds(2 * mm, 2)].reshape(W, W)
        return panel[w, pl.ds(2 * mm, 2)].reshape(W, W)

    def project(x, w):
        for mm in range(N_MP):
            part = jnp.dot(x[mm], block(w, mm), preferred_element_type=F32)
            if mm == 0:
                acc[...] = part
            else:
                acc[...] += part
        return acc[...].astype(BF16)

    got_x(0)
    hops = ((2, 0), (-2, 2 * SPAN))
    for kv, w in ((0, 0), (1, 2)):
        win[SPAN, kv] = project(gx.at[0], w).reshape(OWN_DEV, RET, W)
        for e, (o, there) in enumerate(hops):
            go(remote(win.at[SPAN, kv], win.at[there, kv], k_send.at[kv, e], k_recv.at[kv, e], near(o), m_id))
        go(remote(win.at[SPAN, kv], win.at[1 + 2 * core, kv], k_send.at[kv, 2], k_recv.at[kv, 2], sibling, m_id))

    ring_step(1, 4)

    got_x(2)
    gain_copy.wait()
    for dm in (1, 2, 3):
        remote(gg.at[0], gg.at[0], g_send.at[dm], g_recv.at[dm], s_id, m_id).wait_recv()

    @pl.loop(0, 4)
    def _(b):
        rows = pl.ds(pl.multiple_of(b * 64, 64), 64)
        total = jnp.zeros((64, HD), F32)
        for mm in range(N_MP):
            x = gx[2, mm, rows, :].astype(F32)
            x = x * x
            total = total + (x[:, :128] + x[:, 128:256] + x[:, 256:])
        scale = lax.rsqrt(jnp.sum(total, axis=1, keepdims=True) * (1.0 / D) + epsilon)
        inv[rows, :] = jnp.broadcast_to(scale, (64, HD))
        for mm in range(N_MP):
            x = gx[2, mm, rows, :].astype(F32)
            nx[mm, rows, :] = (x * scale * gg[mm, 0:1, :]).astype(BF16)

    got_shared(1)
    for w in (1, 3):
        for yy in range(NY):
            begin = 24 * yy // 16 * 16
            rows = panel[w, :, begin:begin + 32, :].reshape(8 * 32, W)
            ordered[w // 2, yy] = jnp.dot(perm_ref[1 + yy % 2], rows, preferred_element_type=F32).astype(BF16)

    def forward(kv):
        come = 2 * SPAN * (1 - core)
        remote(win.at[SPAN, kv], win.at[come, kv], k_send.at[kv, 1 - core], k_recv.at[kv, 1 - core],
               s_id, m_id).wait_recv()
        go(remote(win.at[come, kv], win.at[3 - 2 * core, kv], k_send.at[kv, 3], k_recv.at[kv, 3], sibling, m_id))

    qs[...] = project(nx, 3)
    forward(0)
    got_x(1)
    da[...] = project(gx.at[1], 1)
    forward(1)
    for kv in (0, 1):
        remote(win.at[SPAN, kv], win.at[SPAN, kv], k_send.at[kv, core], k_recv.at[kv, core], s_id, m_id).wait_recv()
        for e in (2, 3):
            remote(win.at[SPAN, kv], win.at[SPAN, kv], k_send.at[kv, e], k_recv.at[kv, e], s_id, m_id).wait_recv()

    score_scale = HD ** (-0.5)

    def rows_of(kv, c, h):
        cols = pl.ds(h * HD, HD)
        parts = []
        for j in range(2):
            slot = slot_ref[2 * c + j]
            parts.append(win[slot // 2, kv, slot % 2, :, cols])
        return jnp.concatenate(parts, axis=0)

    pairs = [(c, h) for c in range(CH) for h in range(HEADS)]
    for c, h in pairs:
        r, cols = pl.ds(c * STRETCH, STRETCH), pl.ds(h * HD, HD)
        scores = lax.dot_general(qs[r, cols], rows_of(0, c, h), NT, preferred_element_type=F32) * score_scale
        e = jnp.exp(scores - jnp.max(scores, axis=1, keepdims=True))
        weights = e / jnp.sum(e, axis=1, keepdims=True)
        wts[c * HEADS + h] = weights
        weights_low = weights.astype(BF16)
        for j in range(2):
            wl[h, j, r, :] = weights_low[:, j * RET:(j + 1) * RET]
        att[r, cols] = jnp.dot(weights_low, rows_of(1, c, h), preferred_element_type=F32).astype(BF16)

    right_mp, left_mp = lax.rem(m_id + 1, N_MP), lax.rem(m_id + 3, N_MP)
    top, bottom = pl.ds(0, T // 2), pl.ds(T // 2, T // 2)

    def move(b, e, src, dst, to):
        go(remote(src, dst, p_send.at[b, e], p_recv.at[b, e], s_id, to))

    def moved(b, e):
        remote(rly.at[b, 0], rly.at[b, 0], p_send.at[b, e], p_recv.at[b, e], s_id, m_id).wait_recv()

    def send_piece(b, dm, piece):
        if dm == 0:
            mine[b] = piece
            return
        sb[b, dm - 1] = piece
        if dm == 2:
            move(b, 0, sb.at[b, 1, top], rly.at[b, 0], right_mp)
            move(b, 1, sb.at[b, 1, bottom], rly.at[b, 1], left_mp)
        elif dm == 1:
            move(b, 2, sb.at[b, 0, bottom], rb.at[b, 0, bottom], right_mp)
        else:
            move(b, 3, sb.at[b, 2, top], rb.at[b, 1, top], left_mp)

    def relay(b):
        moved(b, 0)
        sb[b, 0, top] = (sb[b, 0, top].astype(F32) + rly[b, 0].astype(F32)).astype(BF16)
        move(b, 4, sb.at[b, 0, top], rb.at[b, 0, top], right_mp)
        moved(b, 1)
        sb[b, 2, bottom] = (sb[b, 2, bottom].astype(F32) + rly[b, 1].astype(F32)).astype(BF16)
        move(b, 5, sb.at[b, 2, bottom], rb.at[b, 1, bottom], left_mp)

    def gather_piece(b):
        for e in (2, 3, 4, 5):
            moved(b, e)

    for dm in (2, 1, 3, 0):
        to = lax.rem(m_id + dm, N_MP)
        piece = lax.dot_general(att[...], block(1, to), NT, preferred_element_type=F32)
        send_piece(0, dm, piece.astype(BF16))

    for c, h in pairs:
        r, cols = pl.ds(c * STRETCH, STRETCH), pl.ds(h * HD, HD)
        weights = wts[c * HEADS + h]
        d_weights = lax.dot_general(da[r, cols], rows_of(1, c, h), NT, preferred_element_type=F32)
        inner = jnp.sum(d_weights * weights, axis=1, keepdims=True)
        d_scores = (weights * (d_weights - inner) * score_scale).astype(BF16)
        for j in range(2):
            ds[h, j, r, :] = d_scores[:, j * RET:(j + 1) * RET]
        dq[r, cols] = jnp.dot(d_scores, rows_of(0, c, h), preferred_element_type=F32).astype(BF16)

    relay(0)

    for kv, left, right in ((0, ds, qs), (1, wl, da)):
        for h in range(HEADS):
            cols = pl.ds(h * HD, HD)
            for c in range(CH):
                rows = right[pl.ds(c * STRETCH, STRETCH), cols]
                for j in range(2):
                    slot = slot_ref[2 * c + j]
                    for s in range(SLOTS):
                        keep = (slot == s).astype(F32).astype(BF16)
                        qm[pl.ds(j * T + c * STRETCH, STRETCH), pl.ds(s * HD, HD)] = rows * keep
            grads = lax.dot_general(left[h].reshape(2 * T, RET), qm[...], TN, preferred_element_type=F32)
            for s in range(SLOTS):
                part = grads[:, s * HD:(s + 1) * HD]
                if s // 2 == SPAN:
                    own[kv, s % 2, :, cols] = part
                else:
                    dwin[s // 2, kv, s % 2, :, cols] = part.astype(BF16)
        for e, (src, dst, to) in enumerate((
            (dwin.at[1 + 2 * core, kv], rs.at[1, kv], sibling),
            (dwin.at[2 * SPAN * core, kv], rg.at[1 - core, kv], near(4 * core - 2)),
            (dwin.at[3 - 2 * core, kv], rs.at[0, kv], sibling),
        )):
            go(remote(src, dst, v_send.at[kv, e], v_recv.at[kv, e], to, m_id))

    def returned(kv, e):
        remote(rs.at[0, kv], rs.at[0, kv], v_send.at[kv, e], v_recv.at[kv, e], s_id, m_id).wait_recv()

    def join(kv):
        returned(kv, 0)
        here = dwin.at[2 * SPAN * (1 - core), kv]
        for l in range(OWN_DEV):
            dsum[kv, l] = (here[l].astype(F32) + rs[1, kv, l].astype(F32)).astype(BF16)
        go(remote(dsum.at[kv], rg.at[core, kv], v_send.at[kv, 3], v_recv.at[kv, 3], near(2 - 4 * core), m_id))

    join(0)

    acc[:, :HD] = jnp.zeros((T, HD), F32)
    for dm in (2, 1, 3, 0):
        to = lax.rem(m_id + dm, N_MP)
        piece = lax.dot_general(dq[...], block(3, to), NT, preferred_element_type=F32).astype(BF16)
        send_piece(1, dm, piece)
        prod = gx[2, to].astype(F32) * gg[to, 0:1, :] * piece.astype(F32)
        acc[:, :HD] += prod[:, :128] + prod[:, 128:256] + prod[:, 256:]
    join(1)
    relay(1)
    st[...] = jnp.broadcast_to(jnp.sum(acc[:, :HD].T, axis=0, keepdims=True), (8, T))
    for dm in (1, 2, 3):
        go(remote(st, so.at[dm - 1], s_send.at[dm], s_recv.at[dm], s_id, lax.rem(m_id + dm, N_MP)))

    def total(b, rows):
        value = mine[b, rows, :].astype(F32)
        for i in range(2):
            value = value + rb[b, i, rows, :].astype(F32)
        return value

    gather_piece(0)

    @pl.loop(0, 4)
    def _(b):
        rows = pl.ds(pl.multiple_of(b * 64, 64), 64)
        outs[0, rows, :] = total(0, rows).astype(BF16)

    out0 = pltpu.make_async_copy(outs.at[0], bout_ref, osem.at[0])
    out0.start()

    for kv in (0, 1):
        for e in (1, 2, 3):
            returned(kv, e)
        for l in range(OWN_DEV):
            value = own[kv, l]
            for part in (rs.at[0], rg.at[0], rg.at[1]):
                value = value + part[kv, l].astype(F32)
            low[kv, pl.ds(l * RET, RET), :] = value.astype(BF16)
    for dm in (2, 1, 3, 0):
        to = lax.rem(m_id + dm, N_MP)
        acc[...] = lax.dot_general(low[0], block(0, to), NT, preferred_element_type=F32)
        acc[...] += lax.dot_general(low[1], block(2, to), NT, preferred_element_type=F32)
        send_piece(2, dm, acc[...].astype(BF16))

    gather_piece(1)
    for dm in (1, 2, 3):
        remote(st, so.at[dm - 1], s_send.at[dm], s_recv.at[dm], s_id, m_id).wait_recv()
    stat = st[0:1, :] + so[0, 0:1, :] + so[1, 0:1, :] + so[2, 0:1, :]
    acc[:, :HD] = jnp.broadcast_to(stat * (1.0 / D), (HD, T)).T

    @pl.loop(0, 4)
    def _(b):
        rows = pl.ds(pl.multiple_of(b * 64, 64), 64)
        d_normed = total(1, rows)
        scale = inv[rows, :]
        scale = jnp.concatenate([scale] * 3, axis=1)
        mean = acc[rows, :HD]
        mean = jnp.concatenate([mean] * 3, axis=1)
        x = gx[2, m_id, rows, :].astype(F32)
        value = scale * gg[m_id, 0:1, :] * d_normed - x * (scale * scale * scale) * mean
        outs[1, rows, :] = value.astype(BF16)

    out1 = pltpu.make_async_copy(outs.at[1], grow_ref, osem.at[1])
    out1.start()

    relay(2)
    gather_piece(2)

    @pl.loop(0, 4)
    def _(b):
        rows = pl.ds(pl.multiple_of(b * 64, 64), 64)
        outs[2, rows, :] = total(2, rows).astype(BF16)

    out2 = pltpu.make_async_copy(outs.at[2], genc_ref, osem.at[2])
    out2.start()
    for copy in sends:
        copy.wait_send()
    out0.wait()
    out1.wait()
    out2.wait()


def layer(slots, hidden_rows, grad_out, encodings, gain, stacked, perm):
    dma = pltpu.SemaphoreType.DMA
    v = pltpu.VMEM
    any_ = pl.BlockSpec(memory_space=pl.ANY)
    out = jax.ShapeDtypeStruct((T, W), BF16)
    return pl.pallas_call(
        kernel,
        out_shape=(out, out, out),
        in_specs=[pl.BlockSpec(memory_space=pltpu.SMEM)] + [any_] * 5 + [pl.BlockSpec(memory_space=pltpu.VMEM)],
        out_specs=(any_, any_, any_),
        scratch_shapes=[
            v((3, N_MP, T, W), BF16),
            v((N_MP, 8, W), F32),
            v((2, 2, PAD, W), BF16),
            v((2, NZ, 2, PAD, W), BF16),
            v((4, NY, 16 * SHARD, W), BF16),
            v((2, NY, 16 * SHARD, W), BF16),
            v((N_MP, T, W), BF16),
            v((T, HD), F32),
            v((T, W), F32),
            v((T, W), BF16),
            v((T, W), BF16),
            v((WIN, 2, OWN_DEV, RET, W), BF16),
            v((CH * HEADS, STRETCH, 2 * RET), F32),
            v((HEADS, 2, T, RET), BF16),
            v((HEADS, 2, T, RET), BF16),
            v((2 * T, SLOTS * HD), BF16),
            v((WIN, 2, OWN_DEV, RET, W), BF16),
            v((2, OWN_DEV, RET, W), F32),
            v((2, 2, OWN_DEV, RET, W), BF16),
            v((2, OWN_DEV, RET, W), BF16),
            v((2, 2, OWN_DEV, RET, W), BF16),
            v((T, W), BF16),
            v((T, W), BF16),
            v((2, T, W), BF16),
            v((3, 3, T, W), BF16),
            v((3, 2, T // 2, W), BF16),
            v((3, 2, T, W), BF16),
            v((3, T, W), BF16),
            v((8, T), F32),
            v((3, 8, T), F32),
            v((3, T, W), BF16),
            dma((2,)), dma((2,)),
            dma((2, 8)), dma((2, 8)),
            dma((3, 4)), dma((3, 4)),
            dma((4,)), dma((4,)),
            dma((2, 2, 10)), dma((2, 2, 10)),
            dma((2, NY)), dma((2, NY)),
            dma((2, 4)), dma((2, 4)),
            dma((2, 4)), dma((2, 4)),
            dma((3, 6)), dma((3, 6)),
            dma((4,)), dma((4,)),
            dma((7,)), dma((3,)),
        ],
        compiler_params=pltpu.CompilerParams(
            collective_id=0, has_side_effects=True, vmem_limit_bytes=56 << 20
        ),
    )(slots, hidden_rows, grad_out, encodings, gain, stacked, perm)


def shards(hidden_rows, norm_gain, encodings, w_query, w_key, w_value, w_out, neighbours, grad_out):
    device = lax.axis_index("seq")
    owners = neighbours // OWN_DEV
    offsets = (owners - device + SPAN) % lax.axis_size("seq")
    slots = (offsets * OWN_DEV + neighbours % OWN_DEV).reshape(-1)
    stacked = jnp.stack([w_key, w_out.T, w_value, w_query], axis=0)
    stacked = jnp.pad(stacked, ((0, 0), (0, PAD - SHARD), (0, 0))).reshape(2, 2, PAD, W)
    gain = jnp.broadcast_to(norm_gain.astype(F32)[None, :], (8, W))
    perm = jnp.asarray(order_matrices(), BF16)
    bout, grow, genc = layer(
        slots, hidden_rows, grad_out, encodings.reshape(T, W), gain, stacked, perm
    )
    return bout, grow, genc.reshape(OWN_DEV, RET, W)


def solution(mesh):
    placed = (
        P("seq", "mp"),
        P("mp"),
        P("seq", None, "mp"),
        P("seq", "mp"),
        P("seq", "mp"),
        P("seq", "mp"),
        P("mp", "seq"),
        P("seq", None),
        P("seq", "mp"),
    )
    return jax.shard_map(
        shards,
        mesh=mesh,
        in_specs=placed,
        out_specs=(P("seq", "mp"), P("seq", "mp"), P("seq", None, "mp")),
        check_vma=False,
    )
```

```python
import jax
import jax.numpy as jnp
import numpy as np
from jax import lax
from jax.experimental import pallas as pl
from jax.experimental.pallas import tpu as pltpu
from jax.sharding import PartitionSpec as P

HD = 128
STRETCH = 64
RET = 128
SPAN = 2
OWN_DEV = 2
NY = 8
NZ = 8
N_MP = 4
HEADS = 3
WIN = 2 * SPAN + 1
SLOTS = WIN * OWN_DEV
W = 384
D = 1536
SHARD = 12
PAD = 16
T = 256
CH = 4
F32 = jnp.float32
BF16 = jnp.bfloat16
MESH = pl.DeviceIdType.MESH
NT = (((1,), (1,)), ((), ()))
TN = (((0,), (0,)), ((), ()))
epsilon = 1e-05


def order_matrices():
    rows = np.arange(16 * SHARD)
    columns = np.arange(2 * W // 3)[None, :]
    padded = (rows // SHARD) * PAD + rows % SHARD
    pair = 2 * SHARD
    even = (rows // pair) * 32 + rows % pair
    return np.stack([columns == source[:, None] for source in (padded, even, even + 8)]).astype(np.float32)


def kernel(
    slot_ref, hid_ref, grad_ref, enc_ref, gain_ref, ws_ref, perm_ref,
    bout_ref, grow_ref, genc_ref,
    gx, gg, pair, stage, panel, ordered, nx, inv, acc, qs, da, win, wts, wl, ds, qm, dwin, own, rs, dsum, rg,
    att, dq, low, sb, rly, rb, mine, st, so,
    a_send, a_recv, z_send, z_recv, x_send, x_recv, g_send, g_recv, r_send, r_recv, b_send, b_recv,
    k_send, k_recv, v_send, v_recv, p_send, p_recv, s_send, s_recv, loc,
):
    s_id = lax.axis_index("seq")
    m_id = lax.axis_index("mp")
    core = lax.rem(s_id, 2)
    z_id = lax.rem(s_id // 2, NZ)
    y_id = s_id // (2 * NZ)

    def sid(y, z, c):
        return (lax.rem(y + NY, NY) * NZ + lax.rem(z + NZ, NZ)) * 2 + lax.rem(c, 2)

    def near(o):
        return lax.rem(s_id + o + 2 * NY * NZ, 2 * NY * NZ)

    def remote(src, dst, ssem, rsem, seq, mp):
        return pltpu.make_async_remote_copy(
            src_ref=src, dst_ref=dst, send_sem=ssem, recv_sem=rsem,
            device_id=(seq, mp), device_id_type=MESH,
        )

    barrier = pltpu.get_barrier_semaphore()
    sibling = sid(y_id, z_id, core + 1)
    place_of = (z_id, y_id)

    def peer(i, e):
        return sid(y_id, z_id + e, core) if i == 0 else sid(y_id + e, z_id, core)

    greeted = [(sibling, m_id)]
    greeted += [(peer(i, e), m_id) for i in (0, 1) for e in range(1, NZ)]
    greeted += [(near(2), m_id), (near(-2), m_id)]
    greeted += [(s_id, lax.rem(m_id + dm, N_MP)) for dm in (1, 2, 3)]
    for who in greeted:
        pl.semaphore_signal(barrier, inc=1, device_id=who, device_id_type=MESH)
    pl.semaphore_wait(barrier, len(greeted))

    sends = []

    def go(copy):
        copy.start()
        sends.append(copy)

    own_shards = []
    for i in (0, 1):
        go(remote(ws_ref.at[1 - core, i], pair.at[i, core], a_send.at[i], a_recv.at[i], sibling, m_id))
        c = pltpu.make_async_copy(ws_ref.at[core, i], pair.at[i, core], loc.at[5 + i])
        c.start()
        own_shards.append(c)

    locals_ = {}
    for t, ref in ((0, enc_ref), (2, hid_ref), (1, grad_ref)):
        for dm in (1, 2, 3):
            go(remote(ref, gx.at[t, m_id], x_send.at[t, dm], x_recv.at[t, dm],
                      s_id, lax.rem(m_id + dm, N_MP)))
        c = pltpu.make_async_copy(ref, gx.at[t, m_id], loc.at[1 + t])
        c.start()
        locals_[t] = c
    for dm in (1, 2, 3):
        go(remote(gain_ref, gg.at[m_id], g_send.at[dm], g_recv.at[dm],
                  s_id, lax.rem(m_id + dm, N_MP)))
    gain_copy = pltpu.make_async_copy(gain_ref, gg.at[m_id], loc.at[4])
    gain_copy.start()

    def got_x(t):
        locals_[t].wait()
        for dm in (1, 2, 3):
            remote(gx.at[t, 0], gx.at[t, 0], x_send.at[t, dm], x_recv.at[t, dm], s_id, m_id).wait_recv()

    for i in (0, 1):
        own_shards[i].wait()
        remote(pair.at[i, 0], pair.at[i, 0], a_send.at[i], a_recv.at[i], s_id, m_id).wait_recv()
        for e in (1, 7, 2, 6, 3, 5, 4):
            go(remote(pair.at[i], stage.at[i, place_of[i]], z_send.at[i, e], z_recv.at[i, e], peer(i, e), m_id))
        stage[i, place_of[i]] = pair[i]

    def ring(i, k, step, right):
        place = panel.at[2 * core + i, lax.rem(place_of[1 - i] + k + NY, NY)]
        e = step * 2 + right
        return remote(place, place, r_send.at[i, e], r_recv.at[i, e],
                      peer(1 - i, 1 if right else -1), m_id)

    def share(i, k):
        place = panel.at[2 * core + i, lax.rem(place_of[1 - i] + k + NY, NY)]
        go(remote(place, place, b_send.at[i, k % NY], b_recv.at[i, k % NY], sibling, m_id))

    def last(i, right):
        return 4 if right == (i == 0) else 3

    def ring_start(i):
        for e in range(1, NZ):
            remote(pair.at[i], stage.at[i, 0], z_send.at[i, e], z_recv.at[i, e], s_id, m_id).wait_recv()
        panel[2 * core + i, place_of[1 - i]] = jnp.dot(
            perm_ref[0], stage[i].reshape(16 * PAD, W), preferred_element_type=F32
        ).astype(BF16)
        go(ring(i, 0, 1, 1))
        go(ring(i, 0, 1, 0))
        share(i, 0)

    def ring_step(i, step):
        for right in (1, 0):
            k = -step if right else step
            if step <= last(i, right):
                ring(i, k, step, right).wait_recv()
                if step < last(i, right):
                    go(ring(i, k, step + 1, right))
                share(i, k)

    def got_shared(i):
        for k in range(NY):
            place = panel.at[2 * core + i, k]
            remote(place, place, b_send.at[i, k], b_recv.at[i, k], s_id, m_id).wait_recv()

    ring_start(0)
    ring_start(1)
    for step in (1, 2, 3, 4):
        ring_step(0, step)
        if step < 4:
            ring_step(1, step)
    got_shared(0)

    def block(w, mm):
        if w in (1, 3):
            return ordered[w // 2, pl.ds(2 * mm, 2)].reshape(W, W)
        return panel[w, pl.ds(2 * mm, 2)].reshape(W, W)

    def project(x, w):
        for mm in range(N_MP):
            part = jnp.dot(x[mm], block(w, mm), preferred_element_type=F32)
            if mm == 0:
                acc[...] = part
            else:
                acc[...] += part
        return acc[...].astype(BF16)

    got_x(0)
    hops = ((2, 0), (-2, 2 * SPAN))
    for kv, w in ((0, 0), (1, 2)):
        win[SPAN, kv] = project(gx.at[0], w).reshape(OWN_DEV, RET, W)
        for e, (o, there) in enumerate(hops):
            go(remote(win.at[SPAN, kv], win.at[there, kv], k_send.at[kv, e], k_recv.at[kv, e], near(o), m_id))
        go(remote(win.at[SPAN, kv], win.at[1 + 2 * core, kv], k_send.at[kv, 2], k_recv.at[kv, 2], sibling, m_id))

    ring_step(1, 4)

    got_x(2)
    gain_copy.wait()
    for dm in (1, 2, 3):
        remote(gg.at[0], gg.at[0], g_send.at[dm], g_recv.at[dm], s_id, m_id).wait_recv()

    @pl.loop(0, 4)
    def _(b):
        rows = pl.ds(pl.multiple_of(b * 64, 64), 64)
        total = jnp.zeros((64, HD), F32)
        for mm in range(N_MP):
            x = gx[2, mm, rows, :].astype(F32)
            x = x * x
            total = total + (x[:, :128] + x[:, 128:256] + x[:, 256:])
        scale = lax.rsqrt(jnp.sum(total, axis=1, keepdims=True) * (1.0 / D) + epsilon)
        inv[rows, :] = jnp.broadcast_to(scale, (64, HD))
        for mm in range(N_MP):
            x = gx[2, mm, rows, :].astype(F32)
            nx[mm, rows, :] = (x * scale * gg[mm, 0:1, :]).astype(BF16)

    got_shared(1)
    for w in (1, 3):
        for yy in range(NY):
            begin = 24 * yy // 16 * 16
            rows = panel[w, :, begin:begin + 32, :].reshape(8 * 32, W)
            ordered[w // 2, yy] = jnp.dot(perm_ref[1 + yy % 2], rows, preferred_element_type=F32).astype(BF16)

    def forward(kv):
        come = 2 * SPAN * (1 - core)
        remote(win.at[SPAN, kv], win.at[come, kv], k_send.at[kv, 1 - core], k_recv.at[kv, 1 - core],
               s_id, m_id).wait_recv()
        go(remote(win.at[come, kv], win.at[3 - 2 * core, kv], k_send.at[kv, 3], k_recv.at[kv, 3], sibling, m_id))

    qs[...] = project(nx, 3)
    forward(0)
    got_x(1)
    da[...] = project(gx.at[1], 1)
    forward(1)
    for kv in (0, 1):
        remote(win.at[SPAN, kv], win.at[SPAN, kv], k_send.at[kv, core], k_recv.at[kv, core], s_id, m_id).wait_recv()
        for e in (2, 3):
            remote(win.at[SPAN, kv], win.at[SPAN, kv], k_send.at[kv, e], k_recv.at[kv, e], s_id, m_id).wait_recv()

    score_scale = HD ** (-0.5)

    def rows_of(kv, c, h):
        cols = pl.ds(h * HD, HD)
        parts = []
        for j in range(2):
            slot = slot_ref[2 * c + j]
            parts.append(win[slot // 2, kv, slot % 2, :, cols])
        return jnp.concatenate(parts, axis=0)

    pairs = [(c, h) for c in range(CH) for h in range(HEADS)]
    for c, h in pairs:
        r, cols = pl.ds(c * STRETCH, STRETCH), pl.ds(h * HD, HD)
        scores = lax.dot_general(qs[r, cols], rows_of(0, c, h), NT, preferred_element_type=F32) * score_scale
        e = jnp.exp(scores - jnp.max(scores, axis=1, keepdims=True))
        weights = e / jnp.sum(e, axis=1, keepdims=True)
        wts[c * HEADS + h] = weights
        weights_low = weights.astype(BF16)
        for j in range(2):
            wl[h, j, r, :] = weights_low[:, j * RET:(j + 1) * RET]
        att[r, cols] = jnp.dot(weights_low, rows_of(1, c, h), preferred_element_type=F32).astype(BF16)

    right_mp, left_mp = lax.rem(m_id + 1, N_MP), lax.rem(m_id + 3, N_MP)
    top, bottom = pl.ds(0, T // 2), pl.ds(T // 2, T // 2)

    def move(b, e, src, dst, to):
        go(remote(src, dst, p_send.at[b, e], p_recv.at[b, e], s_id, to))

    def moved(b, e):
        remote(rly.at[b, 0], rly.at[b, 0], p_send.at[b, e], p_recv.at[b, e], s_id, m_id).wait_recv()

    def send_piece(b, dm, piece):
        if dm == 0:
            mine[b] = piece
            return
        sb[b, dm - 1] = piece
        if dm == 2:
            move(b, 0, sb.at[b, 1, top], rly.at[b, 0], right_mp)
            move(b, 1, sb.at[b, 1, bottom], rly.at[b, 1], left_mp)
        elif dm == 1:
            move(b, 2, sb.at[b, 0, bottom], rb.at[b, 0, bottom], right_mp)
        else:
            move(b, 3, sb.at[b, 2, top], rb.at[b, 1, top], left_mp)

    def relay(b):
        moved(b, 0)
        sb[b, 0, top] = (sb[b, 0, top].astype(F32) + rly[b, 0].astype(F32)).astype(BF16)
        move(b, 4, sb.at[b, 0, top], rb.at[b, 0, top], right_mp)
        moved(b, 1)
        sb[b, 2, bottom] = (sb[b, 2, bottom].astype(F32) + rly[b, 1].astype(F32)).astype(BF16)
        move(b, 5, sb.at[b, 2, bottom], rb.at[b, 1, bottom], left_mp)

    def gather_piece(b):
        for e in (2, 3, 4, 5):
            moved(b, e)

    for dm in (2, 1, 3, 0):
        to = lax.rem(m_id + dm, N_MP)
        piece = lax.dot_general(att[...], block(1, to), NT, preferred_element_type=F32)
        send_piece(0, dm, piece.astype(BF16))

    for c, h in pairs:
        r, cols = pl.ds(c * STRETCH, STRETCH), pl.ds(h * HD, HD)
        weights = wts[c * HEADS + h]
        d_weights = lax.dot_general(da[r, cols], rows_of(1, c, h), NT, preferred_element_type=F32)
        inner = jnp.sum(d_weights * weights, axis=1, keepdims=True)
        d_scores = (weights * (d_weights - inner) * score_scale).astype(BF16)
        for j in range(2):
            ds[h, j, r, :] = d_scores[:, j * RET:(j + 1) * RET]
        dq[r, cols] = jnp.dot(d_scores, rows_of(0, c, h), preferred_element_type=F32).astype(BF16)

    relay(0)

    for kv, left, right in ((0, ds, qs), (1, wl, da)):
        for h in range(HEADS):
            cols = pl.ds(h * HD, HD)
            for c in range(CH):
                rows = right[pl.ds(c * STRETCH, STRETCH), cols]
                for j in range(2):
                    slot = slot_ref[2 * c + j]
                    for s in range(SLOTS):
                        keep = (slot == s).astype(F32).astype(BF16)
                        qm[pl.ds(j * T + c * STRETCH, STRETCH), pl.ds(s * HD, HD)] = rows * keep
            grads = lax.dot_general(left[h].reshape(2 * T, RET), qm[...], TN, preferred_element_type=F32)
            for s in range(SLOTS):
                part = grads[:, s * HD:(s + 1) * HD]
                if s // 2 == SPAN:
                    own[kv, s % 2, :, cols] = part
                else:
                    dwin[s // 2, kv, s % 2, :, cols] = part.astype(BF16)
        for e, (src, dst, to) in enumerate((
            (dwin.at[1 + 2 * core, kv], rs.at[1, kv], sibling),
            (dwin.at[2 * SPAN * core, kv], rg.at[1 - core, kv], near(4 * core - 2)),
            (dwin.at[3 - 2 * core, kv], rs.at[0, kv], sibling),
        )):
            go(remote(src, dst, v_send.at[kv, e], v_recv.at[kv, e], to, m_id))

    def returned(kv, e):
        remote(rs.at[0, kv], rs.at[0, kv], v_send.at[kv, e], v_recv.at[kv, e], s_id, m_id).wait_recv()

    def join(kv):
        returned(kv, 0)
        here = dwin.at[2 * SPAN * (1 - core), kv]
        for l in range(OWN_DEV):
            dsum[kv, l] = (here[l].astype(F32) + rs[1, kv, l].astype(F32)).astype(BF16)
        go(remote(dsum.at[kv], rg.at[core, kv], v_send.at[kv, 3], v_recv.at[kv, 3], near(2 - 4 * core), m_id))

    join(0)

    acc[:, :HD] = jnp.zeros((T, HD), F32)
    for dm in (2, 1, 3, 0):
        to = lax.rem(m_id + dm, N_MP)
        piece = lax.dot_general(dq[...], block(3, to), NT, preferred_element_type=F32).astype(BF16)
        send_piece(1, dm, piece)
        prod = gx[2, to].astype(F32) * gg[to, 0:1, :] * piece.astype(F32)
        acc[:, :HD] += prod[:, :128] + prod[:, 128:256] + prod[:, 256:]
    join(1)
    relay(1)
    st[...] = jnp.broadcast_to(jnp.sum(acc[:, :HD].T, axis=0, keepdims=True), (8, T))
    for dm in (1, 2, 3):
        go(remote(st, so.at[dm - 1], s_send.at[dm], s_recv.at[dm], s_id, lax.rem(m_id + dm, N_MP)))

    def total(b, rows):
        value = mine[b, rows, :].astype(F32)
        for i in range(2):
            value = value + rb[b, i, rows, :].astype(F32)
        return value

    gather_piece(0)

    @pl.loop(0, 4)
    def _(b):
        rows = pl.ds(pl.multiple_of(b * 64, 64), 64)
        bout_ref[rows, :] = total(0, rows).astype(BF16)


    for kv in (0, 1):
        for e in (1, 2, 3):
            returned(kv, e)
        for l in range(OWN_DEV):
            value = own[kv, l]
            for part in (rs.at[0], rg.at[0], rg.at[1]):
                value = value + part[kv, l].astype(F32)
            low[kv, pl.ds(l * RET, RET), :] = value.astype(BF16)
    for dm in (2, 1, 3, 0):
        to = lax.rem(m_id + dm, N_MP)
        acc[...] = lax.dot_general(low[0], block(0, to), NT, preferred_element_type=F32)
        acc[...] += lax.dot_general(low[1], block(2, to), NT, preferred_element_type=F32)
        send_piece(2, dm, acc[...].astype(BF16))

    gather_piece(1)
    for dm in (1, 2, 3):
        remote(st, so.at[dm - 1], s_send.at[dm], s_recv.at[dm], s_id, m_id).wait_recv()
    stat = st[0:1, :] + so[0, 0:1, :] + so[1, 0:1, :] + so[2, 0:1, :]
    acc[:, :HD] = jnp.broadcast_to(stat * (1.0 / D), (HD, T)).T

    @pl.loop(0, 4)
    def _(b):
        rows = pl.ds(pl.multiple_of(b * 64, 64), 64)
        d_normed = total(1, rows)
        scale = inv[rows, :]
        scale = jnp.concatenate([scale] * 3, axis=1)
        mean = acc[rows, :HD]
        mean = jnp.concatenate([mean] * 3, axis=1)
        x = gx[2, m_id, rows, :].astype(F32)
        value = scale * gg[m_id, 0:1, :] * d_normed - x * (scale * scale * scale) * mean
        grow_ref[rows, :] = value.astype(BF16)


    relay(2)
    gather_piece(2)

    @pl.loop(0, 4)
    def _(b):
        rows = pl.ds(pl.multiple_of(b * 64, 64), 64)
        genc_ref[rows, :] = total(2, rows).astype(BF16)

    for copy in sends:
        copy.wait_send()


def layer(slots, hidden_rows, grad_out, encodings, gain, stacked, perm):
    dma = pltpu.SemaphoreType.DMA
    v = pltpu.VMEM
    any_ = pl.BlockSpec(memory_space=pl.ANY)
    vmem = pl.BlockSpec(memory_space=pltpu.VMEM)
    hbm = pl.BlockSpec(memory_space=pltpu.HBM)
    out = jax.ShapeDtypeStruct((T, W), BF16)
    return pl.pallas_call(
        kernel,
        out_shape=(out, out, out),
        in_specs=[pl.BlockSpec(memory_space=pltpu.SMEM)] + [hbm] * 3 + [any_] * 2 + [pl.BlockSpec(memory_space=pltpu.VMEM)],
        out_specs=(vmem, vmem, vmem),
        scratch_shapes=[
            v((3, N_MP, T, W), BF16),
            v((N_MP, 8, W), F32),
            v((2, 2, PAD, W), BF16),
            v((2, NZ, 2, PAD, W), BF16),
            v((4, NY, 16 * SHARD, W), BF16),
            v((2, NY, 16 * SHARD, W), BF16),
            v((N_MP, T, W), BF16),
            v((T, HD), F32),
            v((T, W), F32),
            v((T, W), BF16),
            v((T, W), BF16),
            v((WIN, 2, OWN_DEV, RET, W), BF16),
            v((CH * HEADS, STRETCH, 2 * RET), F32),
            v((HEADS, 2, T, RET), BF16),
            v((HEADS, 2, T, RET), BF16),
            v((2 * T, SLOTS * HD), BF16),
            v((WIN, 2, OWN_DEV, RET, W), BF16),
            v((2, OWN_DEV, RET, W), F32),
            v((2, 2, OWN_DEV, RET, W), BF16),
            v((2, OWN_DEV, RET, W), BF16),
            v((2, 2, OWN_DEV, RET, W), BF16),
            v((T, W), BF16),
            v((T, W), BF16),
            v((2, T, W), BF16),
            v((3, 3, T, W), BF16),
            v((3, 2, T // 2, W), BF16),
            v((3, 2, T, W), BF16),
            v((3, T, W), BF16),
            v((8, T), F32),
            v((3, 8, T), F32),
            dma((2,)), dma((2,)),
            dma((2, 8)), dma((2, 8)),
            dma((3, 4)), dma((3, 4)),
            dma((4,)), dma((4,)),
            dma((2, 10)), dma((2, 10)),
            dma((2, NY)), dma((2, NY)),
            dma((2, 4)), dma((2, 4)),
            dma((2, 4)), dma((2, 4)),
            dma((3, 6)), dma((3, 6)),
            dma((4,)), dma((4,)),
            dma((7,)),
        ],
        compiler_params=pltpu.CompilerParams(
            collective_id=0, has_side_effects=True, vmem_limit_bytes=54500 << 10
        ),
    )(slots, hidden_rows, grad_out, encodings, gain, stacked, perm)


def shards(hidden_rows, norm_gain, encodings, w_query, w_key, w_value, w_out, neighbours, grad_out):
    device = lax.axis_index("seq")
    owners = neighbours // OWN_DEV
    offsets = (owners - device + SPAN) % lax.axis_size("seq")
    slots = (offsets * OWN_DEV + neighbours % OWN_DEV).reshape(-1)
    stacked = jnp.stack([w_key, w_out.T, w_value, w_query], axis=0)
    stacked = jnp.pad(stacked, ((0, 0), (0, PAD - SHARD), (0, 0))).reshape(2, 2, PAD, W)
    gain = jnp.broadcast_to(norm_gain.astype(F32)[None, :], (8, W))
    perm = jnp.asarray(order_matrices(), BF16)
    bout, grow, genc = layer(
        slots, hidden_rows, grad_out, encodings.reshape(T, W), gain, stacked, perm
    )
    return bout, grow, genc.reshape(OWN_DEV, RET, W)


def solution(mesh):
    placed = (
        P("seq", "mp"),
        P("mp"),
        P("seq", None, "mp"),
        P("seq", "mp"),
        P("seq", "mp"),
        P("seq", "mp"),
        P("mp", "seq"),
        P("seq", None),
        P("seq", "mp"),
    )
    return jax.shard_map(
        shards,
        mesh=mesh,
        in_specs=placed,
        out_specs=(P("seq", "mp"), P("seq", "mp"), P("seq", None, "mp")),
        check_vma=False,
    )
```

```python
import jax
import jax.numpy as jnp
import numpy as np
from jax import lax
from jax.experimental import pallas as pl
from jax.experimental.pallas import tpu as pltpu
from jax.sharding import PartitionSpec as P

HD = 128
STRETCH = 64
RET = 128
SPAN = 2
OWN_DEV = 2
NY = 8
NZ = 8
N_MP = 4
HEADS = 3
WIN = 2 * SPAN + 1
SLOTS = WIN * OWN_DEV
W = 384
D = 1536
SHARD = 12
PAD = 16
T = 256
CH = 4
F32 = jnp.float32
BF16 = jnp.bfloat16
MESH = pl.DeviceIdType.MESH
NT = (((1,), (1,)), ((), ()))
TN = (((0,), (0,)), ((), ()))
epsilon = 1e-05


def order_matrices():
    rows = np.arange(16 * SHARD)
    columns = np.arange(2 * W // 3)[None, :]
    padded = (rows // SHARD) * PAD + rows % SHARD
    pair = 2 * SHARD
    even = (rows // pair) * 32 + rows % pair
    return np.stack([columns == source[:, None] for source in (padded, even, even + 8)]).astype(np.float32)


def kernel(
    slot_ref, hid_ref, grad_ref, enc_ref, gain_ref, ws_ref, perm_ref,
    bout_ref, grow_ref, genc_ref,
    gx, gg, pair, stage, panel, ordered, nx, inv, acc, qs, da, win, wts, wl, ds, qm, dwin, own, rs, dsum, rg,
    att, dq, low, sb, rly, rb, mine, st, so,
    a_send, a_recv, z_send, z_recv, x_send, x_recv, g_send, g_recv, r_send, r_recv, b_send, b_recv,
    k_send, k_recv, v_send, v_recv, p_send, p_recv, s_send, s_recv, loc,
):
    s_id = lax.axis_index("seq")
    m_id = lax.axis_index("mp")
    core = lax.rem(s_id, 2)
    z_id = lax.rem(s_id // 2, NZ)
    y_id = s_id // (2 * NZ)

    def sid(y, z, c):
        return (lax.rem(y + NY, NY) * NZ + lax.rem(z + NZ, NZ)) * 2 + lax.rem(c, 2)

    def near(o):
        return lax.rem(s_id + o + 2 * NY * NZ, 2 * NY * NZ)

    def remote(src, dst, ssem, rsem, seq, mp):
        return pltpu.make_async_remote_copy(
            src_ref=src, dst_ref=dst, send_sem=ssem, recv_sem=rsem,
            device_id=(seq, mp), device_id_type=MESH,
        )

    barrier = pltpu.get_barrier_semaphore()
    sibling = sid(y_id, z_id, core + 1)
    place_of = (z_id, y_id)

    def peer(i, e):
        return sid(y_id, z_id + e, core) if i == 0 else sid(y_id + e, z_id, core)

    greeted = [(sibling, m_id)]
    greeted += [(peer(i, e), m_id) for i in (0, 1) for e in range(1, NZ)]
    greeted += [(near(2), m_id), (near(-2), m_id)]
    greeted += [(s_id, lax.rem(m_id + dm, N_MP)) for dm in (1, 2, 3)]
    for who in greeted:
        pl.semaphore_signal(barrier, inc=1, device_id=who, device_id_type=MESH)
    pl.semaphore_wait(barrier, len(greeted))

    sends = []

    def go(copy):
        copy.start()
        sends.append(copy)

    own_shards = []
    for i in (0, 1):
        go(remote(ws_ref.at[1 - core, i], pair.at[i, core], a_send.at[i], a_recv.at[i], sibling, m_id))
        c = pltpu.make_async_copy(ws_ref.at[core, i], pair.at[i, core], loc.at[5 + i])
        c.start()
        own_shards.append(c)

    locals_ = {}
    for t, ref in ((0, enc_ref), (2, hid_ref), (1, grad_ref)):
        for dm in (1, 2, 3):
            go(remote(ref, gx.at[t, m_id], x_send.at[t, dm], x_recv.at[t, dm],
                      s_id, lax.rem(m_id + dm, N_MP)))
        c = pltpu.make_async_copy(ref, gx.at[t, m_id], loc.at[1 + t])
        c.start()
        locals_[t] = c
    for dm in (1, 2, 3):
        go(remote(gain_ref, gg.at[m_id], g_send.at[dm], g_recv.at[dm],
                  s_id, lax.rem(m_id + dm, N_MP)))
    gain_copy = pltpu.make_async_copy(gain_ref, gg.at[m_id], loc.at[4])
    gain_copy.start()

    def got_x(t):
        locals_[t].wait()
        for dm in (1, 2, 3):
            remote(gx.at[t, 0], gx.at[t, 0], x_send.at[t, dm], x_recv.at[t, dm], s_id, m_id).wait_recv()

    for i in (0, 1):
        own_shards[i].wait()
        remote(pair.at[i, 0], pair.at[i, 0], a_send.at[i], a_recv.at[i], s_id, m_id).wait_recv()
        for e in (1, 7, 2, 6, 3, 5, 4):
            go(remote(pair.at[i], stage.at[i, place_of[i]], z_send.at[i, e], z_recv.at[i, e], peer(i, e), m_id))
        stage[i, place_of[i]] = pair[i]

    def ring(i, k, step, right):
        place = panel.at[2 * core + i, lax.rem(place_of[1 - i] + k + NY, NY)]
        e = step * 2 + right
        return remote(place, place, r_send.at[i, e], r_recv.at[i, e],
                      peer(1 - i, 1 if right else -1), m_id)

    def share(i, k):
        place = panel.at[2 * core + i, lax.rem(place_of[1 - i] + k + NY, NY)]
        go(remote(place, place, b_send.at[i, k % NY], b_recv.at[i, k % NY], sibling, m_id))

    def last(i, right):
        return 4 if right == (i == 0) else 3

    def ring_start(i):
        for e in range(1, NZ):
            remote(pair.at[i], stage.at[i, 0], z_send.at[i, e], z_recv.at[i, e], s_id, m_id).wait_recv()
        panel[2 * core + i, place_of[1 - i]] = jnp.dot(
            perm_ref[0], stage[i].reshape(16 * PAD, W), preferred_element_type=F32
        ).astype(BF16)
        go(ring(i, 0, 1, 1))
        go(ring(i, 0, 1, 0))
        share(i, 0)

    def ring_step(i, step):
        for right in (1, 0):
            k = -step if right else step
            if step <= last(i, right):
                ring(i, k, step, right).wait_recv()
                if step < last(i, right):
                    go(ring(i, k, step + 1, right))
                share(i, k)

    def got_shared(i):
        for k in range(NY):
            place = panel.at[2 * core + i, k]
            remote(place, place, b_send.at[i, k], b_recv.at[i, k], s_id, m_id).wait_recv()

    ring_start(0)
    ring_start(1)
    for step in (1, 2, 3, 4):
        ring_step(0, step)
        if step < 4:
            ring_step(1, step)
    got_shared(0)

    def block(w, mm):
        if w in (1, 3):
            return ordered[w // 2, pl.ds(2 * mm, 2)].reshape(W, W)
        return panel[w, pl.ds(2 * mm, 2)].reshape(W, W)

    def project(x, w):
        for mm in range(N_MP):
            part = jnp.dot(x[mm], block(w, mm), preferred_element_type=F32)
            if mm == 0:
                acc[...] = part
            else:
                acc[...] += part
        return acc[...].astype(BF16)

    got_x(0)
    hops = ((2, 0), (-2, 2 * SPAN))
    for kv, w in ((0, 0), (1, 2)):
        win[SPAN, kv] = project(gx.at[0], w).reshape(OWN_DEV, RET, W)
        for e, (o, there) in enumerate(hops):
            go(remote(win.at[SPAN, kv], win.at[there, kv], k_send.at[kv, e], k_recv.at[kv, e], near(o), m_id))
        go(remote(win.at[SPAN, kv], win.at[1 + 2 * core, kv], k_send.at[kv, 2], k_recv.at[kv, 2], sibling, m_id))

    ring_step(1, 4)

    got_x(2)
    gain_copy.wait()
    for dm in (1, 2, 3):
        remote(gg.at[0], gg.at[0], g_send.at[dm], g_recv.at[dm], s_id, m_id).wait_recv()

    @pl.loop(0, 4)
    def _(b):
        rows = pl.ds(pl.multiple_of(b * 64, 64), 64)
        total = jnp.zeros((64, HD), F32)
        for mm in range(N_MP):
            x = gx[2, mm, rows, :].astype(F32)
            x = x * x
            total = total + (x[:, :128] + x[:, 128:256] + x[:, 256:])
        scale = lax.rsqrt(jnp.sum(total, axis=1, keepdims=True) * (1.0 / D) + epsilon)
        inv[rows, :] = jnp.broadcast_to(scale, (64, HD))
        for mm in range(N_MP):
            x = gx[2, mm, rows, :].astype(F32)
            nx[mm, rows, :] = (x * scale * gg[mm, 0:1, :]).astype(BF16)

    got_shared(1)
    for w in (1, 3):
        for yy in range(NY):
            begin = 24 * yy // 16 * 16
            rows = panel[w, :, begin:begin + 32, :].reshape(8 * 32, W)
            ordered[w // 2, yy] = jnp.dot(perm_ref[1 + yy % 2], rows, preferred_element_type=F32).astype(BF16)

    def forward(kv):
        come = 2 * SPAN * (1 - core)
        remote(win.at[SPAN, kv], win.at[come, kv], k_send.at[kv, 1 - core], k_recv.at[kv, 1 - core],
               s_id, m_id).wait_recv()
        go(remote(win.at[come, kv], win.at[3 - 2 * core, kv], k_send.at[kv, 3], k_recv.at[kv, 3], sibling, m_id))

    qs[...] = project(nx, 3)
    forward(0)
    got_x(1)
    da[...] = project(gx.at[1], 1)
    forward(1)
    for kv in (0, 1):
        remote(win.at[SPAN, kv], win.at[SPAN, kv], k_send.at[kv, core], k_recv.at[kv, core], s_id, m_id).wait_recv()
        for e in (2, 3):
            remote(win.at[SPAN, kv], win.at[SPAN, kv], k_send.at[kv, e], k_recv.at[kv, e], s_id, m_id).wait_recv()

    score_scale = HD ** (-0.5)

    def rows_of(kv, c, h):
        cols = pl.ds(h * HD, HD)
        parts = []
        for j in range(2):
            slot = slot_ref[c, j]
            parts.append(win[slot // 2, kv, slot % 2, :, cols])
        return jnp.concatenate(parts, axis=0)

    pairs = [(c, h) for c in range(CH) for h in range(HEADS)]
    for c, h in pairs:
        r, cols = pl.ds(c * STRETCH, STRETCH), pl.ds(h * HD, HD)
        scores = lax.dot_general(qs[r, cols], rows_of(0, c, h), NT, preferred_element_type=F32) * score_scale
        e = jnp.exp(scores - jnp.max(scores, axis=1, keepdims=True))
        weights = e * (1.0 / jnp.sum(e, axis=1, keepdims=True))
        wts[c * HEADS + h] = weights
        weights_low = weights.astype(BF16)
        for j in range(2):
            wl[h, j, r, :] = weights_low[:, j * RET:(j + 1) * RET]
        att[r, cols] = jnp.dot(weights_low, rows_of(1, c, h), preferred_element_type=F32).astype(BF16)

    right_mp, left_mp = lax.rem(m_id + 1, N_MP), lax.rem(m_id + 3, N_MP)
    top, bottom = pl.ds(0, T // 2), pl.ds(T // 2, T // 2)

    def move(b, e, src, dst, to):
        go(remote(src, dst, p_send.at[b, e], p_recv.at[b, e], s_id, to))

    def moved(b, e):
        remote(rly.at[b, 0], rly.at[b, 0], p_send.at[b, e], p_recv.at[b, e], s_id, m_id).wait_recv()

    def send_piece(b, dm, piece):
        if dm == 0:
            mine[b] = piece
            return
        sb[b, dm - 1] = piece
        if dm == 2:
            move(b, 0, sb.at[b, 1, top], rly.at[b, 0], right_mp)
            move(b, 1, sb.at[b, 1, bottom], rly.at[b, 1], left_mp)
        elif dm == 1:
            move(b, 2, sb.at[b, 0, bottom], rb.at[b, 0, bottom], right_mp)
        else:
            move(b, 3, sb.at[b, 2, top], rb.at[b, 1, top], left_mp)

    def relay(b):
        moved(b, 0)
        sb[b, 0, top] = (sb[b, 0, top].astype(F32) + rly[b, 0].astype(F32)).astype(BF16)
        move(b, 4, sb.at[b, 0, top], rb.at[b, 0, top], right_mp)
        moved(b, 1)
        sb[b, 2, bottom] = (sb[b, 2, bottom].astype(F32) + rly[b, 1].astype(F32)).astype(BF16)
        move(b, 5, sb.at[b, 2, bottom], rb.at[b, 1, bottom], left_mp)

    def gather_piece(b):
        for e in (2, 3, 4, 5):
            moved(b, e)

    for dm in (2, 1, 3, 0):
        to = lax.rem(m_id + dm, N_MP)
        piece = lax.dot_general(att[...], block(1, to), NT, preferred_element_type=F32)
        send_piece(0, dm, piece.astype(BF16))

    for c, h in pairs:
        r, cols = pl.ds(c * STRETCH, STRETCH), pl.ds(h * HD, HD)
        weights = wts[c * HEADS + h]
        d_weights = lax.dot_general(da[r, cols], rows_of(1, c, h), NT, preferred_element_type=F32)
        inner = jnp.sum(d_weights * weights, axis=1, keepdims=True)
        d_scores = (weights * (d_weights - inner) * score_scale).astype(BF16)
        for j in range(2):
            ds[h, j, r, :] = d_scores[:, j * RET:(j + 1) * RET]
        dq[r, cols] = jnp.dot(d_scores, rows_of(0, c, h), preferred_element_type=F32).astype(BF16)

    for kv, left, right in ((0, ds, qs), (1, wl, da)):
        for h in range(HEADS):
            cols = pl.ds(h * HD, HD)
            for c in range(CH):
                rows = right[pl.ds(c * STRETCH, STRETCH), cols]
                for j in range(2):
                    slot = slot_ref[c, j]
                    for s in range(SLOTS):
                        keep = (slot == s).astype(F32).astype(BF16)
                        qm[pl.ds(j * T + c * STRETCH, STRETCH), pl.ds(s * HD, HD)] = rows * keep
            grads = lax.dot_general(left[h].reshape(2 * T, RET), qm[...], TN, preferred_element_type=F32)
            for s in range(SLOTS):
                part = grads[:, s * HD:(s + 1) * HD]
                if s // 2 == SPAN:
                    own[kv, s % 2, :, cols] = part
                else:
                    dwin[s // 2, kv, s % 2, :, cols] = part.astype(BF16)
        for e, (src, dst, to) in enumerate((
            (dwin.at[1 + 2 * core, kv], rs.at[1, kv], sibling),
            (dwin.at[2 * SPAN * core, kv], rg.at[1 - core, kv], near(4 * core - 2)),
            (dwin.at[3 - 2 * core, kv], rs.at[0, kv], sibling),
        )):
            go(remote(src, dst, v_send.at[kv, e], v_recv.at[kv, e], to, m_id))

    def returned(kv, e):
        remote(rs.at[0, kv], rs.at[0, kv], v_send.at[kv, e], v_recv.at[kv, e], s_id, m_id).wait_recv()

    def join(kv):
        returned(kv, 0)
        here = dwin.at[2 * SPAN * (1 - core), kv]
        for l in range(OWN_DEV):
            dsum[kv, l] = (here[l].astype(F32) + rs[1, kv, l].astype(F32)).astype(BF16)
        go(remote(dsum.at[kv], rg.at[core, kv], v_send.at[kv, 3], v_recv.at[kv, 3], near(2 - 4 * core), m_id))

    relay(0)
    join(0)

    acc[:, :HD] = jnp.zeros((T, HD), F32)
    for dm in (2, 1, 3, 0):
        to = lax.rem(m_id + dm, N_MP)
        piece = lax.dot_general(dq[...], block(3, to), NT, preferred_element_type=F32).astype(BF16)
        send_piece(1, dm, piece)
        prod = gx[2, to].astype(F32) * gg[to, 0:1, :] * piece.astype(F32)
        acc[:, :HD] += prod[:, :128] + prod[:, 128:256] + prod[:, 256:]
    join(1)
    relay(1)
    st[...] = jnp.broadcast_to(jnp.sum(acc[:, :HD].T, axis=0, keepdims=True), (8, T))
    for dm in (1, 2, 3):
        go(remote(st, so.at[dm - 1], s_send.at[dm], s_recv.at[dm], s_id, lax.rem(m_id + dm, N_MP)))

    def total(b, rows):
        value = mine[b, rows, :].astype(F32)
        for i in range(2):
            value = value + rb[b, i, rows, :].astype(F32)
        return value

    gather_piece(0)

    @pl.loop(0, 4)
    def _(b):
        rows = pl.ds(pl.multiple_of(b * 64, 64), 64)
        bout_ref[rows, :] = total(0, rows).astype(BF16)


    for kv in (0, 1):
        for e in (1, 2, 3):
            returned(kv, e)
        for l in range(OWN_DEV):
            value = own[kv, l]
            for part in (rs.at[0], rg.at[0], rg.at[1]):
                value = value + part[kv, l].astype(F32)
            low[kv, pl.ds(l * RET, RET), :] = value.astype(BF16)
    for dm in (2, 1, 3, 0):
        to = lax.rem(m_id + dm, N_MP)
        acc[...] = lax.dot_general(low[0], block(0, to), NT, preferred_element_type=F32)
        acc[...] += lax.dot_general(low[1], block(2, to), NT, preferred_element_type=F32)
        send_piece(2, dm, acc[...].astype(BF16))

    gather_piece(1)
    for dm in (1, 2, 3):
        remote(st, so.at[dm - 1], s_send.at[dm], s_recv.at[dm], s_id, m_id).wait_recv()
    stat = st[0:1, :] + so[0, 0:1, :] + so[1, 0:1, :] + so[2, 0:1, :]
    acc[:, :HD] = jnp.broadcast_to(stat * (1.0 / D), (HD, T)).T

    @pl.loop(0, 4)
    def _(b):
        rows = pl.ds(pl.multiple_of(b * 64, 64), 64)
        d_normed = total(1, rows)
        scale = inv[rows, :]
        scale = jnp.concatenate([scale] * 3, axis=1)
        mean = acc[rows, :HD]
        mean = jnp.concatenate([mean] * 3, axis=1)
        x = gx[2, m_id, rows, :].astype(F32)
        value = scale * gg[m_id, 0:1, :] * d_normed - x * (scale * scale * scale) * mean
        grow_ref[rows, :] = value.astype(BF16)


    relay(2)
    gather_piece(2)

    @pl.loop(0, 4)
    def _(b):
        rows = pl.ds(pl.multiple_of(b * 64, 64), 64)
        genc_ref[rows, :] = total(2, rows).astype(BF16)

    for copy in sends:
        copy.wait_send()


def layer(slots, hidden_rows, grad_out, encodings, gain, stacked, perm):
    dma = pltpu.SemaphoreType.DMA
    v = pltpu.VMEM
    any_ = pl.BlockSpec(memory_space=pl.ANY)
    vmem = pl.BlockSpec(memory_space=pltpu.VMEM)
    hbm = pl.BlockSpec(memory_space=pltpu.HBM)
    out = jax.ShapeDtypeStruct((T, W), BF16)
    return pl.pallas_call(
        kernel,
        out_shape=(out, out, out),
        in_specs=[pl.BlockSpec(memory_space=pltpu.SMEM)] + [hbm] * 3 + [any_] * 2 + [pl.BlockSpec(memory_space=pltpu.VMEM)],
        out_specs=(vmem, vmem, vmem),
        scratch_shapes=[
            v((3, N_MP, T, W), BF16),
            v((N_MP, 8, W), F32),
            v((2, 2, PAD, W), BF16),
            v((2, NZ, 2, PAD, W), BF16),
            v((4, NY, 16 * SHARD, W), BF16),
            v((2, NY, 16 * SHARD, W), BF16),
            v((N_MP, T, W), BF16),
            v((T, HD), F32),
            v((T, W), F32),
            v((T, W), BF16),
            v((T, W), BF16),
            v((WIN, 2, OWN_DEV, RET, W), BF16),
            v((CH * HEADS, STRETCH, 2 * RET), F32),
            v((HEADS, 2, T, RET), BF16),
            v((HEADS, 2, T, RET), BF16),
            v((2 * T, SLOTS * HD), BF16),
            v((WIN, 2, OWN_DEV, RET, W), BF16),
            v((2, OWN_DEV, RET, W), F32),
            v((2, 2, OWN_DEV, RET, W), BF16),
            v((2, OWN_DEV, RET, W), BF16),
            v((2, 2, OWN_DEV, RET, W), BF16),
            v((T, W), BF16),
            v((T, W), BF16),
            v((2, T, W), BF16),
            v((3, 3, T, W), BF16),
            v((3, 2, T // 2, W), BF16),
            v((3, 2, T, W), BF16),
            v((3, T, W), BF16),
            v((8, T), F32),
            v((3, 8, T), F32),
            dma((2,)), dma((2,)),
            dma((2, 8)), dma((2, 8)),
            dma((3, 4)), dma((3, 4)),
            dma((4,)), dma((4,)),
            dma((2, 10)), dma((2, 10)),
            dma((2, NY)), dma((2, NY)),
            dma((2, 4)), dma((2, 4)),
            dma((2, 4)), dma((2, 4)),
            dma((3, 6)), dma((3, 6)),
            dma((4,)), dma((4,)),
            dma((7,)),
        ],
        compiler_params=pltpu.CompilerParams(
            collective_id=0, has_side_effects=True, vmem_limit_bytes=54500 << 10
        ),
    )(slots, hidden_rows, grad_out, encodings, gain, stacked, perm)


def shards(hidden_rows, norm_gain, encodings, w_query, w_key, w_value, w_out, neighbours, grad_out):
    device = lax.axis_index("seq")
    owners = neighbours // OWN_DEV
    offsets = (owners - device + SPAN) % lax.axis_size("seq")
    slots = offsets * OWN_DEV + neighbours % OWN_DEV
    stacked = jnp.stack([w_key, w_out.T, w_value, w_query], axis=0)
    stacked = jnp.pad(stacked, ((0, 0), (0, PAD - SHARD), (0, 0))).reshape(2, 2, PAD, W)
    gain = jnp.broadcast_to(norm_gain.astype(F32)[None, :], (8, W))
    perm = jnp.asarray(order_matrices(), BF16)
    bout, grow, genc = layer(
        slots, hidden_rows, grad_out, encodings.reshape(T, W), gain, stacked, perm
    )
    return bout, grow, genc.reshape(OWN_DEV, RET, W)


def solution(mesh):
    placed = (
        P("seq", "mp"),
        P("mp"),
        P("seq", None, "mp"),
        P("seq", "mp"),
        P("seq", "mp"),
        P("seq", "mp"),
        P("mp", "seq"),
        P("seq", None),
        P("seq", "mp"),
    )
    return jax.shard_map(
        shards,
        mesh=mesh,
        in_specs=placed,
        out_specs=(P("seq", "mp"), P("seq", "mp"), P("seq", None, "mp")),
        check_vma=False,
    )
```

```python
import jax
import jax.numpy as jnp
import numpy as np
from jax import lax
from jax.experimental import pallas as pl
from jax.experimental.pallas import tpu as pltpu
from jax.sharding import PartitionSpec as P

HD = 128
STRETCH = 64
RET = 128
SPAN = 2
OWN_DEV = 2
NY = 8
NZ = 8
N_MP = 4
HEADS = 3
WIN = 2 * SPAN + 1
SLOTS = WIN * OWN_DEV
W = 384
D = 1536
SHARD = 12
PAD = 16
T = 256
CH = 4
F32 = jnp.float32
BF16 = jnp.bfloat16
MESH = pl.DeviceIdType.MESH
NT = (((1,), (1,)), ((), ()))
TN = (((0,), (0,)), ((), ()))
epsilon = 1e-05


def order_matrices():
    rows = np.arange(16 * SHARD)
    columns = np.arange(2 * W // 3)[None, :]
    padded = (rows // SHARD) * PAD + rows % SHARD
    pair = 2 * SHARD
    even = (rows // pair) * 32 + rows % pair
    return np.stack([columns == source[:, None] for source in (padded, even, even + 8)]).astype(np.float32)


def kernel(
    slot_ref, hid_ref, grad_ref, enc_ref, gain_ref, ws_ref, perm_ref,
    bout_ref, grow_ref, genc_ref,
    gx, gg, pair, stage, panel, ordered, nx, inv, acc, qs, da, win, wts, wl, ds, qm, dwin, own, rs, dsum, rg,
    att, dq, low, sb, rly, rb, mine, st, so,
    a_send, a_recv, z_send, z_recv, x_send, x_recv, g_send, g_recv, r_send, r_recv, b_send, b_recv,
    k_send, k_recv, v_send, v_recv, p_send, p_recv, s_send, s_recv, loc,
):
    s_id = lax.axis_index("seq")
    m_id = lax.axis_index("mp")
    core = lax.rem(s_id, 2)
    z_id = lax.rem(s_id // 2, NZ)
    y_id = s_id // (2 * NZ)

    def sid(y, z, c):
        return (lax.rem(y + NY, NY) * NZ + lax.rem(z + NZ, NZ)) * 2 + lax.rem(c, 2)

    def near(o):
        return lax.rem(s_id + o + 2 * NY * NZ, 2 * NY * NZ)

    def remote(src, dst, ssem, rsem, seq, mp):
        return pltpu.make_async_remote_copy(
            src_ref=src, dst_ref=dst, send_sem=ssem, recv_sem=rsem,
            device_id=(seq, mp), device_id_type=MESH,
        )

    barrier = pltpu.get_barrier_semaphore()
    sibling = sid(y_id, z_id, core + 1)
    place_of = (z_id, y_id)

    def peer(i, e):
        return sid(y_id, z_id + e, core) if i == 0 else sid(y_id + e, z_id, core)

    greeted = [(sibling, m_id)]
    greeted += [(peer(i, e), m_id) for i in (0, 1) for e in range(1, NZ)]
    greeted += [(s_id, lax.rem(m_id + dm, N_MP)) for dm in (1, 2, 3)]
    for who in greeted:
        pl.semaphore_signal(barrier, inc=1, device_id=who, device_id_type=MESH)
    pl.semaphore_wait(barrier, len(greeted))

    sends = []

    def go(copy):
        copy.start()
        sends.append(copy)

    own_shards = []
    for i in (0, 1):
        go(remote(ws_ref.at[1 - core, i], pair.at[i, core], a_send.at[i], a_recv.at[i], sibling, m_id))
        c = pltpu.make_async_copy(ws_ref.at[core, i], pair.at[i, core], loc.at[5 + i])
        c.start()
        own_shards.append(c)

    locals_ = {}
    for t, ref in ((0, enc_ref), (2, hid_ref), (1, grad_ref)):
        for dm in (1, 2, 3):
            go(remote(ref, gx.at[t, m_id], x_send.at[t, dm], x_recv.at[t, dm],
                      s_id, lax.rem(m_id + dm, N_MP)))
        c = pltpu.make_async_copy(ref, gx.at[t, m_id], loc.at[1 + t])
        c.start()
        locals_[t] = c
    for dm in (1, 2, 3):
        go(remote(gain_ref, gg.at[m_id], g_send.at[dm], g_recv.at[dm],
                  s_id, lax.rem(m_id + dm, N_MP)))
    gain_copy = pltpu.make_async_copy(gain_ref, gg.at[m_id], loc.at[4])
    gain_copy.start()

    def got_x(t):
        locals_[t].wait()
        for dm in (1, 2, 3):
            remote(gx.at[t, 0], gx.at[t, 0], x_send.at[t, dm], x_recv.at[t, dm], s_id, m_id).wait_recv()

    for i in (0, 1):
        own_shards[i].wait()
        remote(pair.at[i, 0], pair.at[i, 0], a_send.at[i], a_recv.at[i], s_id, m_id).wait_recv()
        for e in (1, 7, 2, 6, 3, 5, 4):
            go(remote(pair.at[i], stage.at[i, place_of[i]], z_send.at[i, e], z_recv.at[i, e], peer(i, e), m_id))
        stage[i, place_of[i]] = pair[i]

    def ring(i, k, step, right):
        place = panel.at[2 * core + i, lax.rem(place_of[1 - i] + k + NY, NY)]
        e = step * 2 + right
        return remote(place, place, r_send.at[i, e], r_recv.at[i, e],
                      peer(1 - i, 1 if right else -1), m_id)

    def share(i, k):
        place = panel.at[2 * core + i, lax.rem(place_of[1 - i] + k + NY, NY)]
        go(remote(place, place, b_send.at[i, k % NY], b_recv.at[i, k % NY], sibling, m_id))

    def last(i, right):
        return 4 if right == (i == 0) else 3

    def ring_start(i):
        for e in range(1, NZ):
            remote(pair.at[i], stage.at[i, 0], z_send.at[i, e], z_recv.at[i, e], s_id, m_id).wait_recv()
        panel[2 * core + i, place_of[1 - i]] = jnp.dot(
            perm_ref[0], stage[i].reshape(16 * PAD, W), preferred_element_type=F32
        ).astype(BF16)
        go(ring(i, 0, 1, 1))
        go(ring(i, 0, 1, 0))
        share(i, 0)

    def ring_step(i, step):
        for right in (1, 0):
            k = -step if right else step
            if step <= last(i, right):
                ring(i, k, step, right).wait_recv()
                if step < last(i, right):
                    go(ring(i, k, step + 1, right))
                share(i, k)

    def got_shared(i):
        for k in range(NY):
            place = panel.at[2 * core + i, k]
            remote(place, place, b_send.at[i, k], b_recv.at[i, k], s_id, m_id).wait_recv()

    ring_start(0)
    ring_start(1)
    for step in (1, 2, 3, 4):
        ring_step(0, step)
        if step < 4:
            ring_step(1, step)
    got_shared(0)

    def block(w, mm):
        if w in (1, 3):
            return ordered[w // 2, pl.ds(2 * mm, 2)].reshape(W, W)
        return panel[w, pl.ds(2 * mm, 2)].reshape(W, W)

    def project(x, w):
        for mm in range(N_MP):
            part = jnp.dot(x[mm], block(w, mm), preferred_element_type=F32)
            if mm == 0:
                acc[...] = part
            else:
                acc[...] += part
        return acc[...].astype(BF16)

    got_x(0)
    hops = ((2, 0), (-2, 2 * SPAN))
    for kv, w in ((0, 0), (1, 2)):
        win[SPAN, kv] = project(gx.at[0], w).reshape(OWN_DEV, RET, W)
        for e, (o, there) in enumerate(hops):
            go(remote(win.at[SPAN, kv], win.at[there, kv], k_send.at[kv, e], k_recv.at[kv, e], near(o), m_id))
        go(remote(win.at[SPAN, kv], win.at[1 + 2 * core, kv], k_send.at[kv, 2], k_recv.at[kv, 2], sibling, m_id))

    ring_step(1, 4)

    got_x(2)
    gain_copy.wait()
    for dm in (1, 2, 3):
        remote(gg.at[0], gg.at[0], g_send.at[dm], g_recv.at[dm], s_id, m_id).wait_recv()

    @pl.loop(0, 4)
    def _(b):
        rows = pl.ds(pl.multiple_of(b * 64, 64), 64)
        total = jnp.zeros((64, HD), F32)
        for mm in range(N_MP):
            x = gx[2, mm, rows, :].astype(F32)
            x = x * x
            total = total + (x[:, :128] + x[:, 128:256] + x[:, 256:])
        scale = lax.rsqrt(jnp.sum(total, axis=1, keepdims=True) * (1.0 / D) + epsilon)
        inv[rows, :] = jnp.broadcast_to(scale, (64, HD))
        for mm in range(N_MP):
            x = gx[2, mm, rows, :].astype(F32)
            nx[mm, rows, :] = (x * scale * gg[mm, 0:1, :]).astype(BF16)

    got_shared(1)
    for w in (1, 3):
        for yy in range(NY):
            begin = 24 * yy // 16 * 16
            rows = panel[w, :, begin:begin + 32, :].reshape(8 * 32, W)
            ordered[w // 2, yy] = jnp.dot(perm_ref[1 + yy % 2], rows, preferred_element_type=F32).astype(BF16)

    def forward(kv):
        come = 2 * SPAN * (1 - core)
        remote(win.at[SPAN, kv], win.at[come, kv], k_send.at[kv, 1 - core], k_recv.at[kv, 1 - core],
               s_id, m_id).wait_recv()
        go(remote(win.at[come, kv], win.at[3 - 2 * core, kv], k_send.at[kv, 3], k_recv.at[kv, 3], sibling, m_id))

    qs[...] = project(nx, 3)
    forward(0)
    got_x(1)
    da[...] = project(gx.at[1], 1)
    forward(1)
    for kv in (0, 1):
        remote(win.at[SPAN, kv], win.at[SPAN, kv], k_send.at[kv, core], k_recv.at[kv, core], s_id, m_id).wait_recv()
        for e in (2, 3):
            remote(win.at[SPAN, kv], win.at[SPAN, kv], k_send.at[kv, e], k_recv.at[kv, e], s_id, m_id).wait_recv()

    score_scale = HD ** (-0.5)

    def rows_of(kv, c, h):
        cols = pl.ds(h * HD, HD)
        parts = []
        for j in range(2):
            slot = slot_ref[c, j]
            parts.append(win[slot // 2, kv, slot % 2, :, cols])
        return jnp.concatenate(parts, axis=0)

    pairs = [(c, h) for c in range(CH) for h in range(HEADS)]
    for c, h in pairs:
        r, cols = pl.ds(c * STRETCH, STRETCH), pl.ds(h * HD, HD)
        scores = lax.dot_general(qs[r, cols], rows_of(0, c, h), NT, preferred_element_type=F32) * score_scale
        e = jnp.exp(scores - jnp.max(scores, axis=1, keepdims=True))
        weights = e * (1.0 / jnp.sum(e, axis=1, keepdims=True))
        wts[c * HEADS + h] = weights
        weights_low = weights.astype(BF16)
        for j in range(2):
            wl[h, j, r, :] = weights_low[:, j * RET:(j + 1) * RET]
        att[r, cols] = jnp.dot(weights_low, rows_of(1, c, h), preferred_element_type=F32).astype(BF16)

    right_mp, left_mp = lax.rem(m_id + 1, N_MP), lax.rem(m_id + 3, N_MP)
    top, bottom = pl.ds(0, T // 2), pl.ds(T // 2, T // 2)

    def move(b, e, src, dst, to):
        go(remote(src, dst, p_send.at[b, e], p_recv.at[b, e], s_id, to))

    def moved(b, e):
        remote(rly.at[b, 0], rly.at[b, 0], p_send.at[b, e], p_recv.at[b, e], s_id, m_id).wait_recv()

    def send_piece(b, dm, piece):
        if dm == 0:
            mine[b] = piece
            return
        sb[b, dm - 1] = piece
        if dm == 2:
            move(b, 0, sb.at[b, 1, top], rly.at[b, 0], right_mp)
            move(b, 1, sb.at[b, 1, bottom], rly.at[b, 1], left_mp)
        elif dm == 1:
            move(b, 2, sb.at[b, 0, bottom], rb.at[b, 0, bottom], right_mp)
        else:
            move(b, 3, sb.at[b, 2, top], rb.at[b, 1, top], left_mp)

    def relay(b):
        moved(b, 0)
        sb[b, 0, top] = (sb[b, 0, top].astype(F32) + rly[b, 0].astype(F32)).astype(BF16)
        move(b, 4, sb.at[b, 0, top], rb.at[b, 0, top], right_mp)
        moved(b, 1)
        sb[b, 2, bottom] = (sb[b, 2, bottom].astype(F32) + rly[b, 1].astype(F32)).astype(BF16)
        move(b, 5, sb.at[b, 2, bottom], rb.at[b, 1, bottom], left_mp)

    def gather_piece(b):
        for e in (2, 3, 4, 5):
            moved(b, e)

    for dm in (2, 1, 3, 0):
        to = lax.rem(m_id + dm, N_MP)
        piece = lax.dot_general(att[...], block(1, to), NT, preferred_element_type=F32)
        send_piece(0, dm, piece.astype(BF16))

    for c, h in pairs:
        r, cols = pl.ds(c * STRETCH, STRETCH), pl.ds(h * HD, HD)
        weights = wts[c * HEADS + h]
        d_weights = lax.dot_general(da[r, cols], rows_of(1, c, h), NT, preferred_element_type=F32)
        inner = jnp.sum(d_weights * weights, axis=1, keepdims=True)
        d_scores = (weights * (d_weights - inner) * score_scale).astype(BF16)
        for j in range(2):
            ds[h, j, r, :] = d_scores[:, j * RET:(j + 1) * RET]
        dq[r, cols] = jnp.dot(d_scores, rows_of(0, c, h), preferred_element_type=F32).astype(BF16)

    for kv, left, right in ((0, ds, qs), (1, wl, da)):
        for h in range(HEADS):
            cols = pl.ds(h * HD, HD)
            for c in range(CH):
                rows = right[pl.ds(c * STRETCH, STRETCH), cols]
                for j in range(2):
                    slot = slot_ref[c, j]
                    for s in range(SLOTS):
                        keep = (slot == s).astype(F32).astype(BF16)
                        qm[pl.ds(j * T + c * STRETCH, STRETCH), pl.ds(s * HD, HD)] = rows * keep
            grads = lax.dot_general(left[h].reshape(2 * T, RET), qm[...], TN, preferred_element_type=F32)
            for s in range(SLOTS):
                part = grads[:, s * HD:(s + 1) * HD]
                if s // 2 == SPAN:
                    own[kv, s % 2, :, cols] = part
                else:
                    dwin[s // 2, kv, s % 2, :, cols] = part.astype(BF16)
        for e, (src, dst, to) in enumerate((
            (dwin.at[1 + 2 * core, kv], rs.at[1, kv], sibling),
            (dwin.at[2 * SPAN * core, kv], rg.at[1 - core, kv], near(4 * core - 2)),
            (dwin.at[3 - 2 * core, kv], rs.at[0, kv], sibling),
        )):
            go(remote(src, dst, v_send.at[kv, e], v_recv.at[kv, e], to, m_id))

    def returned(kv, e):
        remote(rs.at[0, kv], rs.at[0, kv], v_send.at[kv, e], v_recv.at[kv, e], s_id, m_id).wait_recv()

    def join(kv):
        returned(kv, 0)
        here = dwin.at[2 * SPAN * (1 - core), kv]
        for l in range(OWN_DEV):
            dsum[kv, l] = (here[l].astype(F32) + rs[1, kv, l].astype(F32)).astype(BF16)
        go(remote(dsum.at[kv], rg.at[core, kv], v_send.at[kv, 3], v_recv.at[kv, 3], near(2 - 4 * core), m_id))

    relay(0)
    join(0)

    acc[:, :HD] = jnp.zeros((T, HD), F32)
    for dm in (2, 1, 3, 0):
        to = lax.rem(m_id + dm, N_MP)
        piece = lax.dot_general(dq[...], block(3, to), NT, preferred_element_type=F32).astype(BF16)
        send_piece(1, dm, piece)
        prod = gx[2, to].astype(F32) * gg[to, 0:1, :] * piece.astype(F32)
        acc[:, :HD] += prod[:, :128] + prod[:, 128:256] + prod[:, 256:]
    join(1)
    relay(1)
    st[...] = jnp.broadcast_to(jnp.sum(acc[:, :HD].T, axis=0, keepdims=True), (8, T))
    for dm in (1, 2, 3):
        go(remote(st, so.at[dm - 1], s_send.at[dm], s_recv.at[dm], s_id, lax.rem(m_id + dm, N_MP)))

    def total(b, rows):
        value = mine[b, rows, :].astype(F32)
        for i in range(2):
            value = value + rb[b, i, rows, :].astype(F32)
        return value

    gather_piece(0)

    @pl.loop(0, 4)
    def _(b):
        rows = pl.ds(pl.multiple_of(b * 64, 64), 64)
        bout_ref[rows, :] = total(0, rows).astype(BF16)


    for kv in (0, 1):
        for e in (1, 2, 3):
            returned(kv, e)
        for l in range(OWN_DEV):
            value = own[kv, l]
            for part in (rs.at[0], rg.at[0], rg.at[1]):
                value = value + part[kv, l].astype(F32)
            low[kv, pl.ds(l * RET, RET), :] = value.astype(BF16)
    for dm in (2, 1, 3, 0):
        to = lax.rem(m_id + dm, N_MP)
        acc[...] = lax.dot_general(low[0], block(0, to), NT, preferred_element_type=F32)
        acc[...] += lax.dot_general(low[1], block(2, to), NT, preferred_element_type=F32)
        send_piece(2, dm, acc[...].astype(BF16))

    gather_piece(1)
    for dm in (1, 2, 3):
        remote(st, so.at[dm - 1], s_send.at[dm], s_recv.at[dm], s_id, m_id).wait_recv()
    stat = st[0:1, :] + so[0, 0:1, :] + so[1, 0:1, :] + so[2, 0:1, :]
    acc[:, :HD] = jnp.broadcast_to(stat * (1.0 / D), (HD, T)).T

    @pl.loop(0, 4)
    def _(b):
        rows = pl.ds(pl.multiple_of(b * 64, 64), 64)
        d_normed = total(1, rows)
        scale = inv[rows, :]
        scale = jnp.concatenate([scale] * 3, axis=1)
        mean = acc[rows, :HD]
        mean = jnp.concatenate([mean] * 3, axis=1)
        x = gx[2, m_id, rows, :].astype(F32)
        value = scale * gg[m_id, 0:1, :] * d_normed - x * (scale * scale * scale) * mean
        grow_ref[rows, :] = value.astype(BF16)


    relay(2)
    gather_piece(2)

    @pl.loop(0, 4)
    def _(b):
        rows = pl.ds(pl.multiple_of(b * 64, 64), 64)
        genc_ref[rows, :] = total(2, rows).astype(BF16)

    for copy in sends:
        copy.wait_send()


def layer(slots, hidden_rows, grad_out, encodings, gain, stacked, perm):
    dma = pltpu.SemaphoreType.DMA
    v = pltpu.VMEM
    any_ = pl.BlockSpec(memory_space=pl.ANY)
    vmem = pl.BlockSpec(memory_space=pltpu.VMEM)
    hbm = pl.BlockSpec(memory_space=pltpu.HBM)
    out = jax.ShapeDtypeStruct((T, W), BF16)
    return pl.pallas_call(
        kernel,
        out_shape=(out, out, out),
        in_specs=[pl.BlockSpec(memory_space=pltpu.SMEM)] + [hbm] * 3 + [any_] * 2 + [pl.BlockSpec(memory_space=pltpu.VMEM)],
        out_specs=(vmem, vmem, vmem),
        scratch_shapes=[
            v((3, N_MP, T, W), BF16),
            v((N_MP, 8, W), F32),
            v((2, 2, PAD, W), BF16),
            v((2, NZ, 2, PAD, W), BF16),
            v((4, NY, 16 * SHARD, W), BF16),
            v((2, NY, 16 * SHARD, W), BF16),
            v((N_MP, T, W), BF16),
            v((T, HD), F32),
            v((T, W), F32),
            v((T, W), BF16),
            v((T, W), BF16),
            v((WIN, 2, OWN_DEV, RET, W), BF16),
            v((CH * HEADS, STRETCH, 2 * RET), F32),
            v((HEADS, 2, T, RET), BF16),
            v((HEADS, 2, T, RET), BF16),
            v((2 * T, SLOTS * HD), BF16),
            v((WIN, 2, OWN_DEV, RET, W), BF16),
            v((2, OWN_DEV, RET, W), F32),
            v((2, 2, OWN_DEV, RET, W), BF16),
            v((2, OWN_DEV, RET, W), BF16),
            v((2, 2, OWN_DEV, RET, W), BF16),
            v((T, W), BF16),
            v((T, W), BF16),
            v((2, T, W), BF16),
            v((3, 3, T, W), BF16),
            v((3, 2, T // 2, W), BF16),
            v((3, 2, T, W), BF16),
            v((3, T, W), BF16),
            v((8, T), F32),
            v((3, 8, T), F32),
            dma((2,)), dma((2,)),
            dma((2, 8)), dma((2, 8)),
            dma((3, 4)), dma((3, 4)),
            dma((4,)), dma((4,)),
            dma((2, 10)), dma((2, 10)),
            dma((2, NY)), dma((2, NY)),
            dma((2, 4)), dma((2, 4)),
            dma((2, 4)), dma((2, 4)),
            dma((3, 6)), dma((3, 6)),
            dma((4,)), dma((4,)),
            dma((7,)),
        ],
        compiler_params=pltpu.CompilerParams(
            collective_id=0, has_side_effects=True, vmem_limit_bytes=54500 << 10
        ),
    )(slots, hidden_rows, grad_out, encodings, gain, stacked, perm)


def shards(hidden_rows, norm_gain, encodings, w_query, w_key, w_value, w_out, neighbours, grad_out):
    device = lax.axis_index("seq")
    owners = neighbours // OWN_DEV
    offsets = (owners - device + SPAN) % lax.axis_size("seq")
    slots = offsets * OWN_DEV + neighbours % OWN_DEV
    stacked = jnp.stack([w_key, w_out.T, w_value, w_query], axis=0)
    stacked = jnp.pad(stacked, ((0, 0), (0, PAD - SHARD), (0, 0))).reshape(2, 2, PAD, W)
    gain = jnp.broadcast_to(norm_gain.astype(F32)[None, :], (8, W))
    perm = jnp.asarray(order_matrices(), BF16)
    bout, grow, genc = layer(
        slots, hidden_rows, grad_out, encodings.reshape(T, W), gain, stacked, perm
    )
    return bout, grow, genc.reshape(OWN_DEV, RET, W)


def solution(mesh):
    placed = (
        P("seq", "mp"),
        P("mp"),
        P("seq", None, "mp"),
        P("seq", "mp"),
        P("seq", "mp"),
        P("seq", "mp"),
        P("mp", "seq"),
        P("seq", None),
        P("seq", "mp"),
    )
    return jax.shard_map(
        shards,
        mesh=mesh,
        in_specs=placed,
        out_specs=(P("seq", "mp"), P("seq", "mp"), P("seq", None, "mp")),
        check_vma=False,
    )
```
